256 devices in a mesh: dp: 2 (over y_hi), fsdp: 16 (over x, y_lo, core), tensor: 8 (over z).
Axes of the slice: x: 4, y: 4 (y_hi: 2, y_lo: 2; y = y_hi * 2 + y_lo), z: 8, core: 2. Of those that a mesh axis runs over, the one named last changes fastest.
Arguments:
- activations: bfloat16 [4096, 8192], P(('dp', 'fsdp'), 'tensor'), may hold values from -6 to 6
- cotangent: bfloat16 [4096, 8192], P(('dp', 'fsdp'), 'tensor'), may hold values from -6 to 6
- up_tiles: bfloat16 [1024, 128, 128], P(('fsdp', 'tensor')), may hold values from -0.1875 to 0.1875
- down_tiles: bfloat16 [1024, 128, 128], P(('fsdp', 'tensor')), may hold values from -0.125 to 0.125
- up_rows: int32 [128, 8], P(None, 'tensor'), may hold values from 0 to 63, as said below
- up_cols: int32 [128, 8], P(None, 'tensor'), may hold values from 0 to 15, as said below
- down_rows: int32 [128, 8], P(None, 'tensor'), may hold values from 0 to 15, as said below
- down_cols: int32 [128, 8], P(None, 'tensor'), may hold values from 0 to 63, as said below
Outputs:
- output: bfloat16 [4096, 8192], P(('dp', 'fsdp'), 'tensor')
- input_grad: bfloat16 [4096, 8192], P(('dp', 'fsdp'), 'tensor')
- up_grad: float32 [1024, 128, 128], P(('fsdp', 'tensor'))
- down_grad: float32 [1024, 128, 128], P(('fsdp', 'tensor'))
The draws below stay inside these ranges and needn't reach their ends.
Inputs may be any that keep to these rules, and one draw needn't show every extreme that they name: `up_rows`: within a column, the up tiles of one hidden-unit block name distinct feature blocks. `up_cols`: every value occurs exactly 8 times in each column. `down_rows`: every value occurs exactly 8 times in each column. `down_cols`: within a column, the down tiles of one hidden-unit block name distinct feature blocks.
All inputs are finite; a program needn't handle non-finite values.
Results may differ from the reference program's by a relative error of at most 0.018.
Values may be sent and summed in bfloat16 or wider, within the bound.
No kernel may reach another device: no remote copies, remote signals or barrier semaphores. Data moves between devices by JAX's collectives and lax.ppermute only.
A program may use at most 128 MiB of HBM per device.

```python
import jax
import jax.numpy as jnp
from jax import lax

D = 8192
FF = 16384
BLOCK = 128
TOK_DEV = 128
TOKENS = 4096
RANK_COLS = 16
COL_TILES = 8
RANK_TILES = 128
TILES = 1024
TILE_DEV = 8
N_FSDP = 16
N_TENSOR = 8


def tile_lists(key):
    model_blocks = D // BLOCK
    ranks_here = TILES // RANK_TILES

    def one_block(block_key, top_here, bottom_here):
        order = jax.random.permutation(block_key, model_blocks).astype(jnp.int32)
        spots = jnp.arange(model_blocks, dtype=jnp.int32)
        top_spot = jnp.sum(jnp.where(order == model_blocks - 1, spots, 0))
        moved = order.at[top_spot].set(order[0]).at[0].set(model_blocks - 1)
        order = jnp.where(top_here, moved, order)
        low_spot = jnp.sum(jnp.where(order == 0, spots, 0))
        moved = order.at[low_spot].set(order[1]).at[1].set(0)
        order = jnp.where(bottom_here, moved, order)
        return order[:COL_TILES]

    def one_rank(rank_key):
        order_key, block_key, pick_key = jax.random.split(rank_key, 3)
        chosen = jax.random.randint(pick_key, (2,), 0, RANK_COLS)
        blocks = jnp.arange(RANK_COLS, dtype=jnp.int32)
        block_keys = jax.random.split(block_key, RANK_COLS)
        table = jax.vmap(one_block)(block_keys, blocks == chosen[0], blocks == chosen[1])
        slots = jax.random.permutation(order_key, RANK_TILES).astype(jnp.int32)
        near_blocks = slots // COL_TILES
        far_blocks = table[near_blocks, slots % COL_TILES]
        return (far_blocks, near_blocks)
    keys = jax.random.split(key, ranks_here)
    far_blocks, near_blocks = jax.vmap(one_rank)(keys)
    return (far_blocks.T.astype(jnp.int32), near_blocks.T.astype(jnp.int32))


def draw_up_rows(key, part):
    return tile_lists(jax.random.fold_in(key, 11))[0]


def draw_up_cols(key, part):
    return tile_lists(jax.random.fold_in(key, 11))[1]


def draw_down_rows(key, part):
    return tile_lists(jax.random.fold_in(key, 12))[1]


def draw_down_cols(key, part):
    return tile_lists(jax.random.fold_in(key, 12))[0]


def block_levels(rng, extent, shards, low, top_value):
    def one(dim, shards_of):
        draws = jax.random.uniform(jax.random.fold_in(jax.random.fold_in(rng, 6), dim), (shards_of,), jnp.float32, low / len(shards), top_value / len(shards))
        return jnp.repeat(jnp.exp(draws), extent[dim] // shards_of).reshape((-1,) + (1,) * (len(extent) - dim - 1))

    level = one(*shards[0])
    for cut in shards[1:]:
        level = level * one(*cut)
    return level


def normal_values(rng, shape, scale, most, cuts=(), kind=jnp.bfloat16):
    values = scale * jax.random.normal(rng, shape, jnp.float32)
    if cuts:
        values = values * block_levels(rng, shape, cuts, -0.22, 0.18)
    return jnp.clip(values, -most, most).astype(kind)


def setup_inputs(seed: int = 0) -> dict:
    streams_of = jax.random.split(jax.random.key(seed), 9)
    activations = normal_values(streams_of[0], (TOKENS, D), 1.0, 6.0, ((0, 32), (1, 8)))
    cotangent = normal_values(streams_of[1], (TOKENS, D), 1.0, 6.0, ((0, 32), (1, 8)))
    up_tiles = normal_values(streams_of[2], (TILES, BLOCK, BLOCK), (D // 8) ** -0.5, 0.1875, ((0, 128),))
    down_tiles = normal_values(streams_of[3], (TILES, BLOCK, BLOCK), (FF // 8) ** -0.5, 0.125, ((0, 128),))
    up_rows = draw_up_rows(jax.random.fold_in(streams_of[8], 71), 0)
    up_cols = draw_up_cols(jax.random.fold_in(streams_of[8], 71), 0)
    down_rows = draw_down_rows(jax.random.fold_in(streams_of[8], 71), 0)
    down_cols = draw_down_cols(jax.random.fold_in(streams_of[8], 71), 0)
    return {"activations": activations, "cotangent": cotangent, "up_tiles": up_tiles, "down_tiles": down_tiles, "up_rows": up_rows, "up_cols": up_cols, "down_rows": down_rows, "down_cols": down_cols}


inv_root_two = 0.7071067811865476
inv_root_tau = 0.3989422804014327


def gelu_parts(values):
    normal_cdf = 0.5 * (1.0 + jax.scipy.special.erf(values * inv_root_two))
    density = inv_root_tau * jnp.exp(-0.5 * values * values)
    return values * normal_cdf, normal_cdf + values * density


def rank_order(tiles):
    shaped = tiles.reshape(N_FSDP, N_TENSOR, TILE_DEV, BLOCK, BLOCK)
    return shaped.transpose(1, 0, 2, 3, 4).reshape(TILES, BLOCK, BLOCK)


def tile_order(grads):
    shaped = grads.reshape(N_TENSOR, N_FSDP, TILE_DEV, BLOCK, BLOCK)
    return shaped.transpose(1, 0, 2, 3, 4).reshape(TILES, BLOCK, BLOCK)


def apply_tiles(acting, tiles, source, target, segments, letters):
    picked = acting.reshape(TOK_DEV, -1, BLOCK)[:, source].astype(jnp.float32)
    product = jnp.einsum(letters, picked, tiles)
    summed = jnp.zeros((TOK_DEV, segments, BLOCK), jnp.float32).at[:, target].add(product)
    return summed.reshape(TOK_DEV, segments * BLOCK)


def rank_total(partial_value):
    shaped = partial_value.reshape(TOK_DEV, N_TENSOR, D)
    rounded = lax.optimization_barrier(shaped.astype(jnp.bfloat16)).astype(jnp.float32)
    return jnp.sum(rounded, axis=1).astype(jnp.bfloat16)


def outer_tiles(left_side, right_side, left_index, right_index):
    left_pick = left_side.reshape(TOK_DEV, -1, BLOCK)[:, left_index].astype(jnp.float32)
    right_pick = right_side.reshape(TOK_DEV, -1, BLOCK)[:, right_index].astype(jnp.float32)
    term = jnp.einsum("tnb,tnc->nbc", left_pick, right_pick)
    return lax.optimization_barrier(term.astype(jnp.bfloat16)).astype(jnp.float32)


def reference(activations, cotangent, up_tiles, down_tiles, up_rows, up_cols, down_rows, down_cols):
    ranks = jnp.repeat(jnp.arange(N_TENSOR, dtype=jnp.int32), RANK_TILES)
    model_blocks = D // BLOCK
    up_far = up_rows.T.reshape(-1).astype(jnp.int32)
    up_near = ranks * RANK_COLS + up_cols.T.reshape(-1).astype(jnp.int32)
    down_near = ranks * RANK_COLS + down_rows.T.reshape(-1).astype(jnp.int32)
    down_far = down_cols.T.reshape(-1).astype(jnp.int32)
    up_wide = ranks * model_blocks + up_far
    down_wide = ranks * model_blocks + down_far
    up_float = rank_order(up_tiles).astype(jnp.float32)
    down_float = rank_order(down_tiles).astype(jnp.float32)
    groups = TOKENS // TOK_DEV

    def step(carry, blocks_in):
        input_block, cot_block = blocks_in
        pre_act = apply_tiles(input_block, up_float, up_far, up_near, FF // BLOCK, "tnb,nbc->tnc")
        gelu_out, gelu_slope = gelu_parts(pre_act)
        hidden = gelu_out.astype(jnp.bfloat16)
        output = rank_total(apply_tiles(hidden, down_float, down_near, down_wide, N_TENSOR * model_blocks, "tnb,nbc->tnc"))
        hidden_grad = apply_tiles(cot_block, down_float, down_far, down_near, FF // BLOCK, "tnb,ncb->tnc")
        pre_grad = (hidden_grad * gelu_slope).astype(jnp.bfloat16)
        input_grad = rank_total(apply_tiles(pre_grad, up_float, up_near, up_wide, N_TENSOR * model_blocks, "tnb,ncb->tnc"))
        up_term = outer_tiles(input_block, pre_grad, up_far, up_near)
        down_term = outer_tiles(hidden, cot_block, down_near, down_far)
        return (carry[0] + up_term, carry[1] + down_term), (output, input_grad)

    zeros = jnp.zeros((TILES, BLOCK, BLOCK), jnp.float32)
    inputs_split = activations.reshape(groups, TOK_DEV, D)
    cot_split = cotangent.reshape(groups, TOK_DEV, D)
    sums, results = lax.scan(step, (zeros, zeros), (inputs_split, cot_split))
    output = results[0].reshape(TOKENS, D)
    input_grad = results[1].reshape(TOKENS, D)
    return (output, input_grad, tile_order(sums[0]), tile_order(sums[1]))
```

```python
import functools

import jax
import jax.numpy as jnp
from jax import lax
from jax.experimental import pallas as pl
from jax.experimental.pallas import tpu as pltpu
from jax.sharding import PartitionSpec as P

BF = jnp.bfloat16
F32 = jnp.float32
inv_root_two = 0.7071067811865476
inv_root_tau = 0.3989422804014327

B = 128
H = 16
K = 8
NT = 128
VMEM_LIMIT = 56 * 1024 * 1024

SMEM_SPEC = pl.BlockSpec(memory_space=pltpu.SMEM)
VMEM_SPEC = pl.BlockSpec(memory_space=pltpu.VMEM)
ANY_SPEC = pl.BlockSpec(memory_space=pl.ANY)


def gelu_parts(values):
    normal_cdf = 0.5 * (1.0 + lax.erf(values * inv_root_two))
    density = inv_root_tau * jnp.exp(-0.5 * values * values)
    return (values * normal_cdf, normal_cdf + values * density)


def dot(a, b, dims):
    return lax.dot_general(a, b, ((dims[:1], dims[1:]), ((), ())), preferred_element_type=F32)


def plan_kernel(cols_ref, rows_ref, up_ref, down_ref, count):
    for near, order in ((cols_ref, up_ref), (rows_ref, down_ref)):
        for h in range(H):
            count[h] = 0

        def step(j, carry):
            h = near[j]
            c = count[h]
            order[h * K + c] = j
            count[h] = c + 1
            return carry

        lax.fori_loop(0, NT, step, 0)


def plan(cols, rows):
    shape = jax.ShapeDtypeStruct((NT,), jnp.int32)
    return pl.pallas_call(
        plan_kernel,
        out_shape=(shape, shape),
        in_specs=[SMEM_SPEC] * 2,
        out_specs=(SMEM_SPEC, SMEM_SPEC),
        scratch_shapes=[pltpu.SMEM((H,), jnp.int32)],
        name="plan",
    )(cols, rows)


def block(ref, f):
    return ref[f // 8, :, pl.ds(pl.multiple_of((f % 8) * B, B), B)]


class Wide:
    def __init__(self, arrays, places):
        self.arrays, self.places = arrays, places


def wide_copies(places, refs, pos, buf, sems, first):
    copies = []
    for n, (which, index, shift) in enumerate(places):
        slot = shift if isinstance(shift, int) else lax.rem(pos[0] + shift[0] + 8, 8)
        src = refs[which].at[index] if index is not None else refs[which]
        copies.append(pltpu.make_async_copy(src, buf.at[slot], sems.at[first + n]))
    return copies


def tile_copies(places, refs, pos, buf, sems, first):
    copies = []
    for n, (which, index, (dx, dy, dc)) in enumerate(places):
        slot = (
            lax.rem(pos[1] - dx + 4, 4) * 4
            + lax.rem(pos[2] + dy, 2) * 2
            + lax.rem(pos[3] + dc, 2)
        )
        src = refs[which].at[index] if index is not None else refs[which]
        copies.append(
            pltpu.make_async_copy(src, buf.at[pl.ds(slot * 8, 8)], sems.at[first + n])
        )
    return copies


WIDE = pltpu.VMEM((8, B, 8 * B), BF)
TILES = pltpu.VMEM((NT, B, B), BF)
WIDE_ACC = pltpu.VMEM((8, B, 8 * B), F32)


def call(kernel, out_shape, smem, hbm, vmem, scratch, out_specs=None, name=None):
    n_out = len(out_shape)
    return pl.pallas_call(
        kernel,
        out_shape=tuple(out_shape),
        in_specs=[SMEM_SPEC] * len(smem) + [ANY_SPEC] * len(hbm) + [VMEM_SPEC] * len(vmem),
        out_specs=out_specs or (VMEM_SPEC,) * n_out,
        scratch_shapes=scratch,
        compiler_params=pltpu.CompilerParams(vmem_limit_bytes=VMEM_LIMIT),
        name=name,
    )(*smem, *hbm, *vmem)


def start(copies):
    for c in copies:
        c.start()


def finish(copies):
    for c in copies:
        c.wait()


def far_blocks(buf, rows, order, h):
    return jnp.concatenate([block(buf, rows[order[h * K + k]]) for k in range(K)], axis=1)


def forward(order, rows, pos, x, w):
    def kernel(order, rows, pos, *refs):
        x_refs, w_refs = refs[: len(x.arrays)], refs[len(x.arrays) : len(x.arrays) + len(w.arrays)]
        hidden, slope, xbuf, wbuf, sems = refs[len(x.arrays) + len(w.arrays) :]
        copies = wide_copies(x.places, x_refs, pos, xbuf, sems, 0)
        copies += tile_copies(w.places, w_refs, pos, wbuf, sems, len(x.places))
        start(copies)
        finish(copies)

        def step(h, carry):
            lhs = far_blocks(xbuf, rows, order, h)
            rhs = jnp.concatenate([wbuf[order[h * K + k]] for k in range(K)], axis=0)
            act, der = gelu_parts(dot(lhs, rhs, (1, 0)))
            hidden[h] = act.astype(BF)
            slope[h] = der
            return carry

        lax.fori_loop(0, H, step, 0)

    return call(
        kernel,
        (jax.ShapeDtypeStruct((H, B, B), BF), jax.ShapeDtypeStruct((H, B, B), F32)),
        (order, rows, pos),
        (*x.arrays, *w.arrays),
        (),
        [WIDE, TILES, pltpu.SemaphoreType.DMA((len(x.places) + len(w.places),))],
        name="forward",
    )


GRADS = jax.ShapeDtypeStruct((2, 4, 2, 8, B, B), BF)


def grad_place(j, pos):
    owner = j // 8
    dx = lax.rem(owner // 4 - pos[1] + 4, 4)
    dy = lax.rem(lax.rem(owner // 2, 2) + pos[2], 2)
    dc = lax.rem(lax.rem(owner, 2) + pos[3], 2)
    return dc, dx, dy, lax.rem(j, 8)


def down_grads(order, cols, pos, hidden, cot):
    def kernel(order, cols, pos, *refs):
        n = len(cot.arrays)
        c_refs = refs[:n]
        hid, grads, cbuf, sems = refs[n:]
        copies = wide_copies(cot.places, c_refs, pos, cbuf, sems, 0)
        start(copies)
        finish(copies)

        def step(h, carry):
            term = dot(hid[h], far_blocks(cbuf, cols, order, h), (0, 0)).astype(BF)
            for k in range(K):
                grads[grad_place(order[h * K + k], pos)] = term[:, k * B : (k + 1) * B]
            return carry

        lax.fori_loop(0, H, step, 0)

    return call(
        kernel,
        (GRADS,),
        (order, cols, pos),
        cot.arrays,
        (hidden,),
        [WIDE, pltpu.SemaphoreType.DMA((len(cot.places),))],
        name="down_grads",
    )[0]


def pre_grads(down_order, cols, up_order, rows, pos, slope, cot, w, x):
    def kernel(down_order, cols, up_order, rows, pos, *refs):
        nc, nw, nx = len(cot.arrays), len(w.arrays), len(x.arrays)
        c_refs, w_refs, x_refs = refs[:nc], refs[nc : nc + nw], refs[nc + nw : nc + nw + nx]
        slope, pre, grads, cbuf, wbuf, xbuf, sems = refs[nc + nw + nx :]
        first = wide_copies(cot.places, c_refs, pos, cbuf, sems, 0)
        first += tile_copies(w.places, w_refs, pos, wbuf, sems, len(first))
        later = wide_copies(x.places, x_refs, pos, xbuf, sems, len(first))
        start(first)
        start(later)
        finish(first)

        def step(h, carry):
            lhs = far_blocks(cbuf, cols, down_order, h)
            rhs = jnp.concatenate([wbuf[down_order[h * K + k]] for k in range(K)], axis=1)
            pre[h] = (dot(lhs, rhs, (1, 1)) * slope[h]).astype(BF)
            return carry

        lax.fori_loop(0, H, step, 0)
        finish(later)

        def term(h, carry):
            lhs = far_blocks(xbuf, rows, up_order, h)
            out = dot(lhs, pre[h], (0, 0)).astype(BF)
            for k in range(K):
                grads[grad_place(up_order[h * K + k], pos)] = out[k * B : (k + 1) * B]
            return carry

        lax.fori_loop(0, H, term, 0)

    n = len(cot.places) + len(w.places) + len(x.places)
    return call(
        kernel,
        (jax.ShapeDtypeStruct((H, B, B), BF), GRADS),
        (down_order, cols, up_order, rows, pos),
        (*cot.arrays, *w.arrays, *x.arrays),
        (slope,),
        [WIDE, TILES, WIDE, pltpu.SemaphoreType.DMA((n,))],
        name="pre_grads",
    )


def spread(order, far, pos, act, w, transposed, name):
    def kernel(order, far, pos, *refs):
        nw = len(w.arrays)
        act, out, wbuf, acc, sems = refs[nw:]
        copies = tile_copies(w.places, refs[:nw], pos, wbuf, sems, 0)
        start(copies)
        acc[...] = jnp.zeros_like(acc)
        finish(copies)

        def step(h, carry):
            js = [order[h * K + k] for k in range(K)]
            axis = 0 if transposed else 1
            rhs = jnp.concatenate([wbuf[j] for j in js], axis=axis)
            term = dot(act[h], rhs, (1, 1 - axis))
            for k, j in enumerate(js):
                f = far[j]
                at = (f // 8, slice(None), pl.ds(pl.multiple_of((f % 8) * B, B), B))
                acc[at] += term[:, k * B : (k + 1) * B]
            return carry

        lax.fori_loop(0, H, step, 0)
        out[...] = acc[...].astype(BF)

    return call(
        kernel,
        (jax.ShapeDtypeStruct((8, B, 8 * B), BF),),
        (order, far, pos),
        w.arrays,
        (act,),
        [TILES, WIDE_ACC, pltpu.SemaphoreType.DMA((len(w.places),))],
        name=name,
    )[0]


def core_swap(a):
    return lax.ppermute(a, "fsdp", [(i, i ^ 1) for i in range(16)])


def y_swap(a):
    return lax.ppermute(a, "fsdp", [(i, i ^ 2) for i in range(16)])


def x_shift(a, d):
    return lax.ppermute(a, "fsdp", [(i, (i + 4 * d) % 16) for i in range(16)])


def dp_swap(a):
    return lax.ppermute(a, "dp", [(0, 1), (1, 0)])


def gather_tiles(tiles):
    both = jnp.stack([tiles, y_swap(tiles)])
    mine = [both] + [x_shift(both, d) for d in (1, 2, 3)]
    theirs = [core_swap(a) for a in mine]
    arrays, places = [], []
    for dc, group in enumerate((mine, theirs)):
        for dx, a in enumerate(group):
            for dy in range(2):
                places.append((len(arrays), dy, (dx, dy, dc)))
            arrays.append(a)
    return Wide(tuple(arrays), places)


def reduce_tiles(grads):
    sums = []
    for dx in range(4):
        got = core_swap(grads[1, dx])
        sums.append(grads[0, dx].astype(F32) + got.astype(F32))
    total = sums[0]
    for dx in (1, 2, 3):
        total = total + x_shift(sums[dx].astype(BF), dx).astype(F32)
    part = total[0] + y_swap(total[1].astype(BF)).astype(F32)
    part = part.astype(BF)
    return part.astype(F32) + dp_swap(part).astype(F32)


def scatter_features(partial):
    return lax.psum_scatter(partial, "tensor", scatter_dimension=0, tiled=True)[0]


def body(activations, cotangent, up_tiles, down_tiles, up_rows, up_cols, down_rows, down_cols):
    f = lax.axis_index("fsdp")
    pos = jnp.stack([lax.axis_index("tensor"), f // 4, (f // 2) % 2, f % 2]).astype(jnp.int32)
    rows, cols = up_rows[:, 0], down_cols[:, 0]
    up_order, down_order = plan(up_cols[:, 0], down_rows[:, 0])
    pair = lax.all_gather(jnp.stack([activations, cotangent]), "tensor", axis=0, tiled=False)
    x = Wide((pair,), [(0, (z, 0), z) for z in range(8)])
    cot = Wide((pair,), [(0, (z, 1), z) for z in range(8)])
    up = gather_tiles(up_tiles)
    down = gather_tiles(down_tiles)
    hidden, slope = forward(up_order, rows, pos, x, up)
    down_term = down_grads(down_order, cols, pos, hidden, cot)
    pre_grad, up_term = pre_grads(down_order, cols, up_order, rows, pos, slope, cot, down, x)
    partial_out = spread(down_order, cols, pos, hidden, down, False, "out_part")
    partial_in = spread(up_order, rows, pos, pre_grad, up, True, "in_part")
    output = scatter_features(partial_out)
    input_grad = scatter_features(partial_in)
    return (output, input_grad, reduce_tiles(up_term), reduce_tiles(down_term))


def solution(mesh):
    in_specs = (
        P(("dp", "fsdp"), "tensor"),
        P(("dp", "fsdp"), "tensor"),
        P(("fsdp", "tensor"), None, None),
        P(("fsdp", "tensor"), None, None),
        P(None, "tensor"),
        P(None, "tensor"),
        P(None, "tensor"),
        P(None, "tensor"),
    )
    out_specs = (
        P(("dp", "fsdp"), "tensor"),
        P(("dp", "fsdp"), "tensor"),
        P(("fsdp", "tensor"), None, None),
        P(("fsdp", "tensor"), None, None),
    )
    return jax.shard_map(body, mesh=mesh, in_specs=in_specs, out_specs=out_specs, check_vma=False)
```

```python
import functools

import jax
import jax.numpy as jnp
from jax import lax
from jax.experimental import pallas as pl
from jax.experimental.pallas import tpu as pltpu
from jax.sharding import PartitionSpec as P

BF = jnp.bfloat16
F32 = jnp.float32
inv_root_two = 0.7071067811865476
inv_root_tau = 0.3989422804014327

B = 128
H = 16
K = 8
NT = 128
COST = 10_000_000
VMEM_LIMIT = 56 * 1024 * 1024

SMEM_SPEC = pl.BlockSpec(memory_space=pltpu.SMEM)
VMEM_SPEC = pl.BlockSpec(memory_space=pltpu.VMEM)
ANY_SPEC = pl.BlockSpec(memory_space=pl.ANY)


def gelu_parts(values):
    normal_cdf = 0.5 * (1.0 + lax.erf(values * inv_root_two))
    density = inv_root_tau * jnp.exp(-0.5 * values * values)
    return (values * normal_cdf, normal_cdf + values * density)


def dot(a, b, dims):
    return lax.dot_general(a, b, ((dims[:1], dims[1:]), ((), ())), preferred_element_type=F32)


def plan_kernel(cols_ref, rows_ref, up_ref, down_ref, count):
    for near, order in ((cols_ref, up_ref), (rows_ref, down_ref)):
        for h in range(H):
            count[h] = 0

        def step(j, carry):
            h = near[j]
            c = count[h]
            order[h * K + c] = j
            count[h] = c + 1
            return carry

        lax.fori_loop(0, NT, step, 0)


def plan(cols, rows):
    shape = jax.ShapeDtypeStruct((NT,), jnp.int32)
    return pl.pallas_call(
        plan_kernel,
        out_shape=(shape, shape),
        in_specs=[SMEM_SPEC] * 2,
        out_specs=(SMEM_SPEC, SMEM_SPEC),
        scratch_shapes=[pltpu.SMEM((H,), jnp.int32)],
        name="plan",
    )(cols, rows)


def block(ref, f):
    return ref[f >> 3, :, pl.ds(pl.multiple_of((f & 7) * B, B), B)]


class Wide:
    def __init__(self, arrays, places):
        self.arrays, self.places = arrays, places


def wide_copies(places, refs, pos, buf, sems, first):
    copies = []
    for n, (which, index, shift, lines) in enumerate(places):
        slot = shift if isinstance(shift, int) else (pos[0] + shift[0]) & 7
        src = refs[which].at[index] if index is not None else refs[which]
        dst = buf.at[slot] if lines is None else buf.at[slot, pl.ds(*lines)]
        copies.append(pltpu.make_async_copy(src, dst, sems.at[first + n]))
    return copies


def tile_copies(places, refs, pos, buf, sems, first):
    copies = []
    for n, (which, index, (dx, dy, dc)) in enumerate(places):
        slot = ((pos[1] - dx) & 3) * 4 + (pos[2] ^ dy) * 2 + (pos[3] ^ dc)
        src = refs[which].at[index] if index is not None else refs[which]
        copies.append(
            pltpu.make_async_copy(src, buf.at[pl.ds(slot * 8, 8)], sems.at[first + n])
        )
    return copies


WIDE = pltpu.VMEM((8, B, 8 * B), BF)
TILES = pltpu.VMEM((NT, B, B), BF)
WIDE_ACC = pltpu.VMEM((8, B, 8 * B), F32)


def call(kernel, out_shape, smem, hbm, vmem, scratch, out_specs=None, name=None):
    n_out = len(out_shape)
    return pl.pallas_call(
        kernel,
        out_shape=tuple(out_shape),
        in_specs=[SMEM_SPEC] * len(smem) + [ANY_SPEC] * len(hbm) + [VMEM_SPEC] * len(vmem),
        out_specs=out_specs or (VMEM_SPEC,) * n_out,
        scratch_shapes=scratch,
        compiler_params=pltpu.CompilerParams(vmem_limit_bytes=VMEM_LIMIT),
        cost_estimate=pl.CostEstimate(flops=COST, bytes_accessed=COST // 100, transcendentals=0),
        name=name,
    )(*smem, *hbm, *vmem)


def start(copies):
    for c in copies:
        c.start()


def finish(copies):
    for c in copies:
        c.wait()


def far_blocks(buf, rows, order, h):
    return jnp.concatenate([block(buf, rows[order[h * K + k]]) for k in range(K)], axis=1)


def forward(order, rows, pos, x, w):
    def kernel(order, rows, pos, *refs):
        x_refs, w_refs = refs[: len(x.arrays)], refs[len(x.arrays) : len(x.arrays) + len(w.arrays)]
        hidden, slope, xbuf, wbuf, sems = refs[len(x.arrays) + len(w.arrays) :]
        copies = wide_copies(x.places, x_refs, pos, xbuf, sems, 0)
        copies += tile_copies(w.places, w_refs, pos, wbuf, sems, len(x.places))
        start(copies)
        finish(copies)

        def step(h, carry):
            lhs = far_blocks(xbuf, rows, order, h)
            rhs = jnp.concatenate([wbuf[order[h * K + k]] for k in range(K)], axis=0)
            act, der = gelu_parts(dot(lhs, rhs, (1, 0)))
            hidden[h] = act.astype(BF)
            slope[h] = der
            return carry

        lax.fori_loop(0, H, step, 0, unroll=4)

    return call(
        kernel,
        (jax.ShapeDtypeStruct((H, B, B), BF), jax.ShapeDtypeStruct((H, B, B), F32)),
        (order, rows, pos),
        (*x.arrays, *w.arrays),
        (),
        [WIDE, TILES, pltpu.SemaphoreType.DMA((len(x.places) + len(w.places),))],
        name="forward",
    )


def grad_shapes(x_first):
    n, m = (4, 2) if x_first else (2, 4)
    piece = jax.ShapeDtypeStruct((m, 8, B, B), BF)
    return [piece] * n + [jax.ShapeDtypeStruct((n, m, 8, B, B), BF)]


def grad_scratch(x_first):
    n, m = (4, 2) if x_first else (2, 4)
    return pltpu.VMEM((2, n, m, 8, B, B), BF)


def grad_place(j, pos, x_first):
    dc, dx, dy = ((j >> 3) & 1) ^ pos[3], ((j >> 5) - pos[1]) & 3, ((j >> 4) & 1) ^ pos[2]
    return (dc, dx, dy, j & 7) if x_first else (dc, dy, dx, j & 7)


def grad_copies(grads, outs, sems, first):
    n = len(outs) - 1
    copies = [pltpu.make_async_copy(grads.at[1, i], outs[i], sems.at[first + i]) for i in range(n)]
    return copies + [pltpu.make_async_copy(grads.at[0], outs[n], sems.at[first + n])]


def down_grads(order, cols, pos, hidden, cot, x_first):
    shapes = grad_shapes(x_first)

    def kernel(order, cols, pos, *refs):
        n, m = len(cot.arrays), len(shapes)
        c_refs, hid, outs = refs[:n], refs[n], refs[n + 1 : n + 1 + m]
        cbuf, grads, sems = refs[n + 1 + m :]
        copies = wide_copies(cot.places, c_refs, pos, cbuf, sems, 0)
        start(copies)
        finish(copies)

        def step(h, carry):
            term = dot(hid[h], far_blocks(cbuf, cols, order, h), (0, 0)).astype(BF)
            for k in range(K):
                at = grad_place(order[h * K + k], pos, x_first)
                grads[at] = term[:, k * B : (k + 1) * B]
            return carry

        lax.fori_loop(0, H, step, 0, unroll=4)
        copies = grad_copies(grads, outs, sems, len(cot.places))
        start(copies)
        finish(copies)

    return call(
        kernel,
        shapes,
        (order, cols, pos),
        cot.arrays,
        (hidden,),
        [WIDE, grad_scratch(x_first), pltpu.SemaphoreType.DMA((len(cot.places) + len(shapes),))],
        out_specs=(ANY_SPEC,) * len(shapes),
        name="down_grads",
    )


def pre_grads(down_order, cols, up_order, rows, pos, slope, cot, w, x, x_first):
    shapes = grad_shapes(x_first)

    def kernel(down_order, cols, up_order, rows, pos, *refs):
        nc, nw, nx, m = len(cot.arrays), len(w.arrays), len(x.arrays), len(shapes)
        c_refs, w_refs, x_refs = refs[:nc], refs[nc : nc + nw], refs[nc + nw : nc + nw + nx]
        slope, pre = refs[nc + nw + nx : nc + nw + nx + 2]
        outs = refs[nc + nw + nx + 2 : nc + nw + nx + 2 + m]
        cbuf, wbuf, xbuf, grads, sems = refs[nc + nw + nx + 2 + m :]
        first = wide_copies(cot.places, c_refs, pos, cbuf, sems, 0)
        first += tile_copies(w.places, w_refs, pos, wbuf, sems, len(first))
        later = wide_copies(x.places, x_refs, pos, xbuf, sems, len(first))
        start(first)
        start(later)
        finish(first)

        def step(h, carry):
            lhs = far_blocks(cbuf, cols, down_order, h)
            rhs = jnp.concatenate([wbuf[down_order[h * K + k]] for k in range(K)], axis=1)
            pre[h] = (dot(lhs, rhs, (1, 1)) * slope[h]).astype(BF)
            return carry

        lax.fori_loop(0, H, step, 0, unroll=4)
        finish(later)

        def term(h, carry):
            lhs = far_blocks(xbuf, rows, up_order, h)
            out = dot(lhs, pre[h], (0, 0)).astype(BF)
            for k in range(K):
                at = grad_place(up_order[h * K + k], pos, x_first)
                grads[at] = out[k * B : (k + 1) * B]
            return carry

        lax.fori_loop(0, H, term, 0, unroll=4)
        copies = grad_copies(grads, outs, sems, len(first) + len(later))
        start(copies)
        finish(copies)

    n = len(cot.places) + len(w.places) + len(x.places) + len(shapes)
    out = call(
        kernel,
        [jax.ShapeDtypeStruct((H, B, B), BF)] + shapes,
        (down_order, cols, up_order, rows, pos),
        (*cot.arrays, *w.arrays, *x.arrays),
        (slope,),
        [WIDE, TILES, WIDE, grad_scratch(x_first), pltpu.SemaphoreType.DMA((n,))],
        out_specs=(VMEM_SPEC,) + (ANY_SPEC,) * len(shapes),
        name="pre_grads",
    )
    return out[0], out[1:]


RING = (0, 1, 2, 3, 5, 6, 7)


def spread(order, far, pos, act, w, transposed, ring, name):
    def kernel(order, far, pos, *refs):
        nw = len(w.arrays)
        act, outs, (wbuf, acc, sems) = refs[nw], refs[nw + 1 : -3], refs[-3:]
        copies = tile_copies(w.places, refs[:nw], pos, wbuf, sems, 0)
        start(copies)
        acc[...] = jnp.zeros_like(acc)
        finish(copies)

        def step(h, carry):
            js = [order[h * K + k] for k in range(K)]
            axis = 0 if transposed else 1
            rhs = jnp.concatenate([wbuf[j] for j in js], axis=axis)
            term = dot(act[h], rhs, (1, 1 - axis))
            for k, j in enumerate(js):
                f = far[j]
                at = (f >> 3, slice(None), pl.ds(pl.multiple_of((f & 7) * B, B), B))
                acc[at] += term[:, k * B : (k + 1) * B]
            return carry

        lax.fori_loop(0, H, step, 0, unroll=4)
        if ring:
            low, high, rest = outs
            low[...] = acc[(pos[0] + 4) & 7, : B // 2].astype(BF)
            high[...] = acc[(pos[0] + 4) & 7, B // 2 :].astype(BF)
            for n, r in enumerate(RING):
                rest[n] = acc[(pos[0] + r) & 7].astype(BF)
        else:
            outs[0][...] = acc[...].astype(BF)

    half = jax.ShapeDtypeStruct((B // 2, 8 * B), BF)
    return call(
        kernel,
        [half, half, jax.ShapeDtypeStruct((7, B, 8 * B), BF)]
        if ring
        else [jax.ShapeDtypeStruct((8, B, 8 * B), BF)],
        (order, far, pos),
        w.arrays,
        (act,),
        [TILES, WIDE_ACC, pltpu.SemaphoreType.DMA((len(w.places),))],
        name=name,
    )


def core_swap(a):
    return lax.ppermute(a, "fsdp", [(i, i ^ 1) for i in range(16)])


def y_swap(a):
    return lax.ppermute(a, "fsdp", [(i, i ^ 2) for i in range(16)])


def x_shift(a, d):
    return lax.ppermute(a, "fsdp", [(i, (i + 4 * d) % 16) for i in range(16)])


def dp_swap(a):
    return lax.ppermute(a, "dp", [(0, 1), (1, 0)])


def z_up(a):
    return lax.ppermute(a, "tensor", [(i, (i + 1) % 8) for i in range(8)])


def z_down(a):
    return lax.ppermute(a, "tensor", [(i, (i + 7) % 8) for i in range(8)])


def gather_up(tiles, *early):
    both = after(jnp.stack([tiles, y_swap(tiles)]), *early)
    mine = [both] + [x_shift(both, d) for d in (1, 3, 2)]
    arrays = mine + [core_swap(a) for a in mine]
    places = []
    for n in range(8):
        for dy in range(2):
            places.append((n, dy, ((0, 1, 3, 2)[n % 4], dy, n // 4)))
    return Wide(tuple(arrays), places)


def gather_down(tiles):
    mine = [tiles] + [x_shift(tiles, d) for d in (1, 3, 2)]
    mine += [y_swap(a) for a in mine]
    arrays = mine + [core_swap(a) for a in mine]
    places = [(n, None, ((0, 1, 3, 2)[n % 4], (n // 4) % 2, n // 8)) for n in range(16)]
    return Wide(tuple(arrays), places)


def add(a, b):
    return a.astype(F32) + b.astype(F32)


def scatter_features(partial):
    return lax.psum_scatter(partial, "tensor", scatter_dimension=0, tiled=True)[0]


def after(value, *others):
    return lax.optimization_barrier((value, *others))[0]


def body(activations, cotangent, up_tiles, down_tiles, up_rows, up_cols, down_rows, down_cols):
    f = lax.axis_index("fsdp")
    pos = jnp.stack([lax.axis_index("tensor"), f >> 2, (f >> 1) & 1, f & 1]).astype(jnp.int32)
    rows, cols = up_rows[:, 0], down_cols[:, 0]
    up_order, down_order = plan(up_cols[:, 0], down_rows[:, 0])
    pair = lax.all_gather(jnp.stack([activations, cotangent]), "tensor", axis=0, tiled=False)
    x = Wide((pair,), [(0, (z, 0), z, None) for z in range(8)])
    cot = Wide((pair,), [(0, (z, 1), z, None) for z in range(8)])
    up = gather_up(up_tiles, up_order, down_order, pos)
    down = gather_down(down_tiles)

    hidden, slope = forward(up_order, rows, pos, x, up)
    (partial_out,) = spread(down_order, cols, pos, hidden, down, False, False, "out_part")
    output = scatter_features(partial_out)
    slope_b = after(slope, partial_out)
    pre_grad, (up0, up1, up_keep) = pre_grads(
        down_order, cols, up_order, rows, pos, slope_b, cot, down, x, False
    )
    u1, u0 = core_swap(up1), core_swap(up0)
    hidden_b = after(hidden, up_keep)
    down0, down1, down2, down3, down_keep = down_grads(
        down_order, cols, pos, hidden_b, cot, True
    )
    near = add(up_keep[1], u1).astype(BF)
    u_y = y_swap(near)
    d1, d3 = core_swap(down1), core_swap(down3)
    d2, d0 = core_swap(down2), core_swap(down0)
    t1, t3 = add(down_keep[1], d1).astype(BF), add(down_keep[3], d3).astype(BF)
    d_x1, d_x3 = x_shift(t1, 1), x_shift(t3, 3)
    pre_grad_b = after(pre_grad, near, t1, t3)
    low, high, rest = spread(up_order, rows, pos, pre_grad_b, up, True, True, "in_part")

    part = {r: rest[n] for n, r in enumerate(RING)}
    half = B // 2
    z1, w1 = z_up(low), z_down(high)
    t2 = add(down_keep[2], d2).astype(BF)
    d_x2 = x_shift(after(t2, d_x1), 2)
    z2 = jnp.concatenate([add(part[3][:half], z1).astype(BF), part[3][half:]])
    w2 = jnp.concatenate([part[5][:half], add(part[5][half:], w1).astype(BF)])
    z2, w2 = z_up(after(z2, output, d_x1, d_x3)), z_down(after(w2, output, d_x1, d_x3))
    total = (add(up_keep[0], u0) + u_y.astype(F32)).astype(BF)
    u_x1, u_x3 = x_shift(total[1], 1), x_shift(total[3], 3)
    z3, w3 = add(part[2], z2).astype(BF), add(part[6], w2).astype(BF)
    z3, w3 = z_up(after(z3, total, d_x2)), z_down(after(w3, total, d_x2))
    own = add(down_keep[0], d0) + add(d_x1, d_x3) + d_x2.astype(F32)
    d_y = y_swap(own[1].astype(BF))
    u_x2 = x_shift(after(total[2], u_x1), 2)
    down_mine = (own[0] + d_y.astype(F32)).astype(BF)
    z4, w4 = add(part[1], z3).astype(BF), add(part[7], w3).astype(BF)
    z4, w4 = z_up(after(z4, u_x3, down_mine)), z_down(after(w4, u_x3, down_mine))
    d_dp = dp_swap(down_mine)
    up_mine = (total[0].astype(F32) + add(u_x1, u_x3) + u_x2.astype(F32)).astype(BF)
    u_dp = dp_swap(up_mine)
    input_grad = (part[0].astype(F32) + add(z4, w4)).astype(BF)
    return (output, input_grad, add(up_mine, u_dp), add(down_mine, d_dp))


def solution(mesh):
    in_specs = (
        P(("dp", "fsdp"), "tensor"),
        P(("dp", "fsdp"), "tensor"),
        P(("fsdp", "tensor"), None, None),
        P(("fsdp", "tensor"), None, None),
        P(None, "tensor"),
        P(None, "tensor"),
        P(None, "tensor"),
        P(None, "tensor"),
    )
    out_specs = (
        P(("dp", "fsdp"), "tensor"),
        P(("dp", "fsdp"), "tensor"),
        P(("fsdp", "tensor"), None, None),
        P(("fsdp", "tensor"), None, None),
    )
    return jax.shard_map(body, mesh=mesh, in_specs=in_specs, out_specs=out_specs, check_vma=False)
```

```python
import functools

import jax
import jax.numpy as jnp
from jax import lax
from jax.experimental import pallas as pl
from jax.experimental.pallas import tpu as pltpu
from jax.sharding import PartitionSpec as P

BF = jnp.bfloat16
F32 = jnp.float32
inv_root_two = 0.7071067811865476
inv_root_tau = 0.3989422804014327

B = 128
H = 16
K = 8
NT = 128
COST = 10_000_000
UNROLL = 2
VMEM_LIMIT = 56 * 1024 * 1024

SMEM_SPEC = pl.BlockSpec(memory_space=pltpu.SMEM)
VMEM_SPEC = pl.BlockSpec(memory_space=pltpu.VMEM)
ANY_SPEC = pl.BlockSpec(memory_space=pl.ANY)


def gelu_parts(values):
    normal_cdf = 0.5 * (1.0 + lax.erf(values * inv_root_two))
    density = inv_root_tau * jnp.exp(-0.5 * values * values)
    return (values * normal_cdf, normal_cdf + values * density)


def dot(a, b, dims):
    return lax.dot_general(a, b, ((dims[:1], dims[1:]), ((), ())), preferred_element_type=F32)


def plan_kernel(cols_ref, rows_ref, up_ref, down_ref, count):
    for near, order in ((cols_ref, up_ref), (rows_ref, down_ref)):
        for h in range(H):
            count[h] = 0

        def step(j, carry):
            h = near[j]
            c = count[h]
            order[h * K + c] = j
            count[h] = c + 1
            return carry

        lax.fori_loop(0, NT, step, 0)


def plan(cols, rows):
    shape = jax.ShapeDtypeStruct((NT,), jnp.int32)
    return pl.pallas_call(
        plan_kernel,
        out_shape=(shape, shape),
        in_specs=[SMEM_SPEC] * 2,
        out_specs=(SMEM_SPEC, SMEM_SPEC),
        scratch_shapes=[pltpu.SMEM((H,), jnp.int32)],
        name="plan",
    )(cols, rows)


def block(ref, f):
    return ref[f >> 3, :, pl.ds(pl.multiple_of((f & 7) * B, B), B)]


class Wide:
    def __init__(self, arrays, places):
        self.arrays, self.places = arrays, places


def wide_copies(places, refs, pos, buf, sems, first):
    copies = []
    for n, (which, index, shift, lines) in enumerate(places):
        slot = shift if isinstance(shift, int) else (pos[0] + shift[0]) & 7
        src = refs[which].at[index] if index is not None else refs[which]
        dst = buf.at[slot] if lines is None else buf.at[slot, pl.ds(*lines)]
        copies.append(pltpu.make_async_copy(src, dst, sems.at[first + n]))
    return copies


def tile_copies(places, refs, pos, buf, sems, first):
    copies = []
    for n, (which, index, (dx, dy, dc)) in enumerate(places):
        slot = ((pos[1] - dx) & 3) * 4 + (pos[2] ^ dy) * 2 + (pos[3] ^ dc)
        src = refs[which].at[index] if index is not None else refs[which]
        copies.append(
            pltpu.make_async_copy(src, buf.at[pl.ds(slot * 8, 8)], sems.at[first + n])
        )
    return copies


WIDE = pltpu.VMEM((8, B, 8 * B), BF)
TILES = pltpu.VMEM((NT, B, B), BF)
WIDE_ACC = pltpu.VMEM((8, B, 8 * B), F32)


def call(kernel, out_shape, smem, hbm, vmem, scratch, out_specs=None, name=None):
    n_out = len(out_shape)
    return pl.pallas_call(
        kernel,
        out_shape=tuple(out_shape),
        in_specs=[SMEM_SPEC] * len(smem) + [ANY_SPEC] * len(hbm) + [VMEM_SPEC] * len(vmem),
        out_specs=out_specs or (VMEM_SPEC,) * n_out,
        scratch_shapes=scratch,
        compiler_params=pltpu.CompilerParams(vmem_limit_bytes=VMEM_LIMIT),
        cost_estimate=pl.CostEstimate(flops=COST, bytes_accessed=COST // 100, transcendentals=0),
        name=name,
    )(*smem, *hbm, *vmem)


def start(copies):
    for c in copies:
        c.start()


def finish(copies):
    for c in copies:
        c.wait()


def far_blocks(buf, rows, order, h):
    return jnp.concatenate([block(buf, rows[order[h * K + k]]) for k in range(K)], axis=1)


def add_far(acc, far, js, term):
    for k, j in enumerate(js):
        f = far[j]
        at = (f >> 3, slice(None), pl.ds(pl.multiple_of((f & 7) * B, B), B))
        acc[at] += term[:, k * B : (k + 1) * B]


def forward(up_order, rows, down_order, cols, pos, x, up, down):
    def kernel(up_order, rows, down_order, cols, pos, *refs):
        nx, nu, nd = len(x.arrays), len(up.arrays), len(down.arrays)
        x_refs, u_refs, d_refs = refs[:nx], refs[nx : nx + nu], refs[nx + nu : nx + nu + nd]
        hidden, slope, out, xbuf, ubuf, dbuf, acc, sems = refs[nx + nu + nd :]
        first = wide_copies(x.places, x_refs, pos, xbuf, sems, 0)
        first += tile_copies(up.places, u_refs, pos, ubuf, sems, len(first))
        later = tile_copies(down.places, d_refs, pos, dbuf, sems, len(first))
        start(first)
        start(later)
        acc[...] = jnp.zeros_like(acc)
        finish(first)

        def step(h, carry):
            lhs = far_blocks(xbuf, rows, up_order, h)
            rhs = jnp.concatenate([ubuf[up_order[h * K + k]] for k in range(K)], axis=0)
            act, der = gelu_parts(dot(lhs, rhs, (1, 0)))
            hidden[h] = act.astype(BF)
            slope[h] = der
            return carry

        lax.fori_loop(0, H, step, 0, unroll=UNROLL)
        finish(later)

        def spread_step(h, carry):
            js = [down_order[h * K + k] for k in range(K)]
            rhs = jnp.concatenate([dbuf[j] for j in js], axis=1)
            add_far(acc, cols, js, dot(hidden[h], rhs, (1, 0)))
            return carry

        lax.fori_loop(0, H, spread_step, 0, unroll=UNROLL)
        out[...] = acc[...].astype(BF)

    n = len(x.places) + len(up.places) + len(down.places)
    return call(
        kernel,
        (
            jax.ShapeDtypeStruct((H, B, B), BF),
            jax.ShapeDtypeStruct((H, B, B), F32),
            jax.ShapeDtypeStruct((8, B, 8 * B), BF),
        ),
        (up_order, rows, down_order, cols, pos),
        (*x.arrays, *up.arrays, *down.arrays),
        (),
        [WIDE, TILES, TILES, WIDE_ACC, pltpu.SemaphoreType.DMA((n,))],
        name="forward",
    )


def grad_shapes(x_first):
    n, m = (4, 2) if x_first else (2, 4)
    piece = jax.ShapeDtypeStruct((n // 2, m, 8, B, B), BF)
    return [piece] * 2 + [jax.ShapeDtypeStruct((n, m, 8, B, B), BF)]


def grad_scratch(x_first):
    n, m = (4, 2) if x_first else (2, 4)
    return pltpu.VMEM((2, n, m, 8, B, B), BF)


def grad_place(j, pos, x_first):
    dc, dx, dy = ((j >> 3) & 1) ^ pos[3], ((j >> 5) - pos[1]) & 3, ((j >> 4) & 1) ^ pos[2]
    return (dc, (dx + 3) & 3, dy, j & 7) if x_first else (dc, dy, dx, j & 7)


def grad_copies(grads, outs, sems, first):
    n = outs[0].shape[0]
    return [
        pltpu.make_async_copy(grads.at[1, pl.ds(0, n)], outs[0], sems.at[first]),
        pltpu.make_async_copy(grads.at[1, pl.ds(n, n)], outs[1], sems.at[first + 1]),
        pltpu.make_async_copy(grads.at[0], outs[2], sems.at[first + 2]),
    ]


def backward(down_order, cols, up_order, rows, pos, hidden, slope, cot, w, x):
    up_shapes, down_shapes = grad_shapes(False), grad_shapes(True)

    def kernel(down_order, cols, up_order, rows, pos, *refs):
        nc, nw, nx = len(cot.arrays), len(w.arrays), len(x.arrays)
        c_refs, w_refs, x_refs = refs[:nc], refs[nc : nc + nw], refs[nc + nw : nc + nw + nx]
        hidden, slope, pre = refs[nc + nw + nx : nc + nw + nx + 3]
        ups, downs = refs[nc + nw + nx + 3 : -6][:3], refs[nc + nw + nx + 3 : -6][3:]
        cbuf, wbuf, xbuf, up_terms, down_terms, sems = refs[-6:]
        first = wide_copies(cot.places, c_refs, pos, cbuf, sems, 0)
        first += tile_copies(w.places, w_refs, pos, wbuf, sems, len(first))
        later = wide_copies(x.places, x_refs, pos, xbuf, sems, len(first))
        n = len(first) + len(later)
        start(first)
        start(later)
        finish(first)

        def step(h, carry):
            lhs = far_blocks(cbuf, cols, down_order, h)
            rhs = jnp.concatenate([wbuf[down_order[h * K + k]] for k in range(K)], axis=1)
            pre[h] = (dot(lhs, rhs, (1, 1)) * slope[h]).astype(BF)
            return carry

        lax.fori_loop(0, H, step, 0, unroll=UNROLL)
        finish(later)

        def up_term(h, carry):
            lhs = far_blocks(xbuf, rows, up_order, h)
            out = dot(lhs, pre[h], (0, 0)).astype(BF)
            for k in range(K):
                at = grad_place(up_order[h * K + k], pos, False)
                up_terms[at] = out[k * B : (k + 1) * B]
            return carry

        lax.fori_loop(0, H, up_term, 0, unroll=UNROLL)
        up_copies = grad_copies(up_terms, ups, sems, n)
        start(up_copies)

        def down_term(h, carry):
            out = dot(hidden[h], far_blocks(cbuf, cols, down_order, h), (0, 0)).astype(BF)
            for k in range(K):
                at = grad_place(down_order[h * K + k], pos, True)
                down_terms[at] = out[:, k * B : (k + 1) * B]
            return carry

        lax.fori_loop(0, H, down_term, 0, unroll=UNROLL)
        down_copies = grad_copies(down_terms, downs, sems, n + 3)
        start(down_copies)
        finish(up_copies)
        finish(down_copies)

    n = len(cot.places) + len(w.places) + len(x.places) + 6
    out = call(
        kernel,
        [jax.ShapeDtypeStruct((H, B, B), BF)] + up_shapes + down_shapes,
        (down_order, cols, up_order, rows, pos),
        (*cot.arrays, *w.arrays, *x.arrays),
        (hidden, slope),
        [
            WIDE,
            TILES,
            WIDE,
            grad_scratch(False),
            grad_scratch(True),
            pltpu.SemaphoreType.DMA((n,)),
        ],
        out_specs=(VMEM_SPEC,) + (ANY_SPEC,) * 6,
        name="backward",
    )
    return out[0], out[1:4], out[4:]


RING = (0, 1, 2, 3, 6, 7)


def input_part(order, far, pos, act, w):
    def kernel(order, far, pos, *refs):
        nw = len(w.arrays)
        act, up, down, rest, wbuf, acc, sems = refs[nw:]
        copies = tile_copies(w.places, refs[:nw], pos, wbuf, sems, 0)
        start(copies)
        acc[...] = jnp.zeros_like(acc)
        finish(copies)

        def step(h, carry):
            js = [order[h * K + k] for k in range(K)]
            rhs = jnp.concatenate([wbuf[j] for j in js], axis=0)
            add_far(acc, far, js, dot(act[h], rhs, (1, 1)))
            return carry

        lax.fori_loop(0, H, step, 0, unroll=UNROLL)
        up[...] = acc[(pos[0] + 4) & 7].astype(BF)
        down[...] = acc[(pos[0] + 5) & 7].astype(BF)
        for n, r in enumerate(RING):
            rest[n] = acc[(pos[0] + r) & 7].astype(BF)

    one = jax.ShapeDtypeStruct((B, 8 * B), BF)
    return call(
        kernel,
        [one, one, jax.ShapeDtypeStruct((6, B, 8 * B), BF)],
        (order, far, pos),
        w.arrays,
        (act,),
        [TILES, WIDE_ACC, pltpu.SemaphoreType.DMA((len(w.places),))],
        name="input_part",
    )


def core_swap(a):
    return lax.ppermute(a, "fsdp", [(i, i ^ 1) for i in range(16)])


def y_swap(a):
    return lax.ppermute(a, "fsdp", [(i, i ^ 2) for i in range(16)])


def x_shift(a, d):
    return lax.ppermute(a, "fsdp", [(i, (i + 4 * d) % 16) for i in range(16)])


def dp_swap(a):
    return lax.ppermute(a, "dp", [(0, 1), (1, 0)])


def z_up(a):
    return lax.ppermute(a, "tensor", [(i, (i + 1) % 8) for i in range(8)])


def z_down(a):
    return lax.ppermute(a, "tensor", [(i, (i + 7) % 8) for i in range(8)])


def gather_up(tiles, *early):
    both = after(jnp.stack([tiles, y_swap(tiles)]), *early)
    mine = [both] + [x_shift(both, d) for d in (1, 3, 2)]
    arrays = mine + [core_swap(a) for a in mine]
    places = []
    for n in range(8):
        for dy in range(2):
            places.append((n, dy, ((0, 1, 3, 2)[n % 4], dy, n // 4)))
    return Wide(tuple(arrays), places)


def gather_down(tiles, early):
    x1, x3, x2 = (x_shift(tiles, d) for d in (1, 3, 2))
    mine = [jnp.stack([tiles, after(x1, early)]), jnp.stack([x3, after(x2, early)])]
    mine += [y_swap(a) for a in mine]
    arrays = mine + [core_swap(a) for a in mine]
    places = []
    for n in range(8):
        for i in range(2):
            places.append((n, i, ((0, 1, 3, 2)[n % 2 * 2 + i], n // 2 % 2, n // 4)))
    return Wide(tuple(arrays), places)


def add(a, b):
    return a.astype(F32) + b.astype(F32)


def scatter_features(partial):
    return lax.psum_scatter(partial, "tensor", scatter_dimension=0, tiled=True)[0]


def after(value, *others):
    return lax.optimization_barrier((value, *others))[0]


def body(activations, cotangent, up_tiles, down_tiles, up_rows, up_cols, down_rows, down_cols):
    f = lax.axis_index("fsdp")
    pos = jnp.stack([lax.axis_index("tensor"), f >> 2, (f >> 1) & 1, f & 1]).astype(jnp.int32)
    rows, cols = up_rows[:, 0], down_cols[:, 0]
    up_order, down_order = plan(up_cols[:, 0], down_rows[:, 0])
    pair = lax.all_gather(jnp.stack([activations, cotangent]), "tensor", axis=0, tiled=False)
    x = Wide((pair,), [(0, (z, 0), z, None) for z in range(8)])
    cot = Wide((pair,), [(0, (z, 1), z, None) for z in range(8)])
    up = gather_up(up_tiles, up_order, down_order, pos)
    down = gather_down(down_tiles, up.arrays[0])

    hidden, slope, partial_out = forward(up_order, rows, down_order, cols, pos, x, up, down)
    output = scatter_features(partial_out)
    pre_grad, (up0, up1, up_keep), (down12, down30, down_keep) = backward(
        down_order, cols, up_order, rows, pos, hidden, slope, cot, down, x
    )
    u1, u0 = core_swap(up1), core_swap(up0)
    near = add(up_keep[1], u1[0]).astype(BF)
    u_y = y_swap(near)
    d12, d30 = core_swap(down12), core_swap(down30)
    t1, t2 = add(down_keep[0], d12[0]).astype(BF), add(down_keep[1], d12[1]).astype(BF)
    d_x1 = x_shift(t1, 1)
    t3 = add(down_keep[2], d30[0]).astype(BF)
    d_x3 = x_shift(t3, 3)
    pre_grad_b = after(pre_grad, near, t1, t3)
    part4, part5, rest = input_part(up_order, rows, pos, pre_grad_b, up)

    part = {r: rest[n] for n, r in enumerate(RING)}
    z1, w1 = z_up(part4), z_down(part5)
    d_x2 = x_shift(after(t2, d_x1), 2)
    z2, w2 = add(part[3], z1).astype(BF), add(part[6], w1).astype(BF)
    z2, w2 = z_up(after(z2, output, d_x1, d_x3)), z_down(after(w2, output, d_x1, d_x3))
    total = (add(up_keep[0], u0[0]) + u_y.astype(F32)).astype(BF)
    u_x1, u_x3 = x_shift(total[1], 1), x_shift(total[3], 3)
    z3, w3 = add(part[2], z2).astype(BF), add(part[7], w2).astype(BF)
    z3, w3 = z_up(after(z3, total, d_x2)), z_down(after(w3, total, d_x2))
    own = add(down_keep[3], d30[1]) + add(d_x1, d_x3) + d_x2.astype(F32)
    d_y = y_swap(own[1].astype(BF))
    u_x2 = x_shift(after(total[2], u_x1), 2)
    down_mine = (own[0] + d_y.astype(F32)).astype(BF)
    z4 = add(part[1], z3).astype(BF)
    z4 = z_up(after(z4, u_x3))
    d_dp = dp_swap(down_mine)
    up_mine = (total[0].astype(F32) + add(u_x1, u_x3) + u_x2.astype(F32)).astype(BF)
    u_dp = dp_swap(up_mine)
    input_grad = (part[0].astype(F32) + add(z4, w3)).astype(BF)
    return (output, input_grad, add(up_mine, u_dp), add(down_mine, d_dp))


def solution(mesh):
    in_specs = (
        P(("dp", "fsdp"), "tensor"),
        P(("dp", "fsdp"), "tensor"),
        P(("fsdp", "tensor"), None, None),
        P(("fsdp", "tensor"), None, None),
        P(None, "tensor"),
        P(None, "tensor"),
        P(None, "tensor"),
        P(None, "tensor"),
    )
    out_specs = (
        P(("dp", "fsdp"), "tensor"),
        P(("dp", "fsdp"), "tensor"),
        P(("fsdp", "tensor"), None, None),
        P(("fsdp", "tensor"), None, None),
    )
    return jax.shard_map(body, mesh=mesh, in_specs=in_specs, out_specs=out_specs, check_vma=False)
```

```python
import functools

import jax
import jax.numpy as jnp
from jax import lax
from jax.experimental import pallas as pl
from jax.experimental.pallas import tpu as pltpu
from jax.sharding import PartitionSpec as P

BF = jnp.bfloat16
F32 = jnp.float32
inv_root_two = 0.7071067811865476
inv_root_tau = 0.3989422804014327

B = 128
H = 16
K = 8
NT = 128
COST = 10_000_000
UNROLL = 2
VMEM_LIMIT = 56 * 1024 * 1024

SMEM_SPEC = pl.BlockSpec(memory_space=pltpu.SMEM)
VMEM_SPEC = pl.BlockSpec(memory_space=pltpu.VMEM)
ANY_SPEC = pl.BlockSpec(memory_space=pl.ANY)


def gelu_parts(values):
    normal_cdf = 0.5 * (1.0 + lax.erf(values * inv_root_two))
    density = inv_root_tau * jnp.exp(-0.5 * values * values)
    return (values * normal_cdf, normal_cdf + values * density)


def dot(a, b, dims):
    return lax.dot_general(a, b, ((dims[:1], dims[1:]), ((), ())), preferred_element_type=F32)


def plan_kernel(cols_ref, rows_ref, up_ref, down_ref, count):
    for near, order in ((cols_ref, up_ref), (rows_ref, down_ref)):
        for h in range(H):
            count[h] = 0

        def step(j, carry):
            h = near[j]
            c = count[h]
            order[h * K + c] = j
            count[h] = c + 1
            return carry

        lax.fori_loop(0, NT, step, 0)


def plan(cols, rows):
    shape = jax.ShapeDtypeStruct((NT,), jnp.int32)
    return pl.pallas_call(
        plan_kernel,
        out_shape=(shape, shape),
        in_specs=[SMEM_SPEC] * 2,
        out_specs=(SMEM_SPEC, SMEM_SPEC),
        scratch_shapes=[pltpu.SMEM((H,), jnp.int32)],
        name="plan",
    )(cols, rows)


def block(ref, f):
    return ref[f >> 3, :, pl.ds(pl.multiple_of((f & 7) * B, B), B)]


class Wide:
    def __init__(self, arrays, places):
        self.arrays, self.places = arrays, places


def wide_copies(places, refs, pos, buf, sems, first):
    copies = []
    for n, (which, index, shift, lines) in enumerate(places):
        slot = shift if isinstance(shift, int) else (pos[0] + shift[0]) & 7
        src = refs[which].at[index] if index is not None else refs[which]
        dst = buf.at[slot] if lines is None else buf.at[slot, pl.ds(*lines)]
        copies.append(pltpu.make_async_copy(src, dst, sems.at[first + n]))
    return copies


def tile_copies(places, refs, pos, buf, sems, first):
    copies = []
    for n, (which, index, (dx, dy, dc)) in enumerate(places):
        slot = ((pos[1] - dx) & 3) * 4 + (pos[2] ^ dy) * 2 + (pos[3] ^ dc)
        src = refs[which].at[index] if index is not None else refs[which]
        copies.append(
            pltpu.make_async_copy(src, buf.at[pl.ds(slot * 8, 8)], sems.at[first + n])
        )
    return copies


WIDE = pltpu.VMEM((8, B, 8 * B), BF)
TILES = pltpu.VMEM((NT, B, B), BF)
WIDE_ACC = pltpu.VMEM((8, B, 8 * B), F32)


def call(kernel, out_shape, smem, hbm, vmem, scratch, out_specs=None, name=None):
    n_out = len(out_shape)
    return pl.pallas_call(
        kernel,
        out_shape=tuple(out_shape),
        in_specs=[SMEM_SPEC] * len(smem) + [ANY_SPEC] * len(hbm) + [VMEM_SPEC] * len(vmem),
        out_specs=out_specs or (VMEM_SPEC,) * n_out,
        scratch_shapes=scratch,
        compiler_params=pltpu.CompilerParams(vmem_limit_bytes=VMEM_LIMIT),
        cost_estimate=pl.CostEstimate(flops=COST, bytes_accessed=COST // 100, transcendentals=0),
        name=name,
    )(*smem, *hbm, *vmem)


def start(copies):
    for c in copies:
        c.start()


def finish(copies):
    for c in copies:
        c.wait()


def far_blocks(buf, rows, order, h):
    return jnp.concatenate([block(buf, rows[order[h * K + k]]) for k in range(K)], axis=1)


def add_far(acc, far, js, term):
    for k, j in enumerate(js):
        f = far[j]
        at = (f >> 3, slice(None), pl.ds(pl.multiple_of((f & 7) * B, B), B))
        acc[at] += term[:, k * B : (k + 1) * B]


def forward(up_order, rows, down_order, cols, pos, x, up, down):
    def kernel(up_order, rows, down_order, cols, pos, *refs):
        nx, nu, nd = len(x.arrays), len(up.arrays), len(down.arrays)
        x_refs, u_refs, d_refs = refs[:nx], refs[nx : nx + nu], refs[nx + nu : nx + nu + nd]
        hidden, slope, out, xbuf, ubuf, dbuf, acc, sems = refs[nx + nu + nd :]
        first = wide_copies(x.places, x_refs, pos, xbuf, sems, 0)
        first += tile_copies(up.places, u_refs, pos, ubuf, sems, len(first))
        later = tile_copies(down.places, d_refs, pos, dbuf, sems, len(first))
        start(first)
        start(later)
        acc[...] = jnp.zeros_like(acc)
        finish(first)

        def step(h, carry):
            lhs = far_blocks(xbuf, rows, up_order, h)
            rhs = jnp.concatenate([ubuf[up_order[h * K + k]] for k in range(K)], axis=0)
            act, der = gelu_parts(dot(lhs, rhs, (1, 0)))
            hidden[h] = act.astype(BF)
            slope[h] = der
            return carry

        lax.fori_loop(0, H, step, 0, unroll=UNROLL)
        finish(later)

        def spread_step(h, carry):
            js = [down_order[h * K + k] for k in range(K)]
            rhs = jnp.concatenate([dbuf[j] for j in js], axis=1)
            add_far(acc, cols, js, dot(hidden[h], rhs, (1, 0)))
            return carry

        lax.fori_loop(0, H, spread_step, 0, unroll=UNROLL)
        out[...] = acc[...].astype(BF)

    n = len(x.places) + len(up.places) + len(down.places)
    return call(
        kernel,
        (
            jax.ShapeDtypeStruct((H, B, B), BF),
            jax.ShapeDtypeStruct((H, B, B), F32),
            jax.ShapeDtypeStruct((8, B, 8 * B), BF),
        ),
        (up_order, rows, down_order, cols, pos),
        (*x.arrays, *up.arrays, *down.arrays),
        (),
        [WIDE, TILES, TILES, WIDE_ACC, pltpu.SemaphoreType.DMA((n,))],
        name="forward",
    )


def grad_shapes(x_first):
    n, m = (4, 2) if x_first else (2, 4)
    piece = jax.ShapeDtypeStruct((n // 2, m, 8, B, B), BF)
    return [piece] * 2 + [jax.ShapeDtypeStruct((n, m, 8, B, B), BF)]


def grad_scratch(x_first):
    n, m = (4, 2) if x_first else (2, 4)
    return pltpu.VMEM((2, n, m, 8, B, B), BF)


def grad_place(j, pos, x_first):
    dc, dx, dy = ((j >> 3) & 1) ^ pos[3], ((j >> 5) - pos[1]) & 3, ((j >> 4) & 1) ^ pos[2]
    return (dc, (dx + 3) & 3, dy, j & 7) if x_first else (dc, dy, dx, j & 7)


def grad_copies(grads, outs, sems, first):
    n = outs[0].shape[0]
    return [
        pltpu.make_async_copy(grads.at[1, pl.ds(0, n)], outs[0], sems.at[first]),
        pltpu.make_async_copy(grads.at[1, pl.ds(n, n)], outs[1], sems.at[first + 1]),
        pltpu.make_async_copy(grads.at[0], outs[2], sems.at[first + 2]),
    ]


def backward(down_order, cols, up_order, rows, pos, hidden, slope, cot, w, x):
    up_shapes, down_shapes = grad_shapes(False), grad_shapes(True)

    def kernel(down_order, cols, up_order, rows, pos, *refs):
        nc, nw, nx = len(cot.arrays), len(w.arrays), len(x.arrays)
        c_refs, w_refs, x_refs = refs[:nc], refs[nc : nc + nw], refs[nc + nw : nc + nw + nx]
        hidden, slope, pre = refs[nc + nw + nx : nc + nw + nx + 3]
        ups, downs = refs[nc + nw + nx + 3 : -6][:3], refs[nc + nw + nx + 3 : -6][3:]
        cbuf, wbuf, xbuf, up_terms, down_terms, sems = refs[-6:]
        first = wide_copies(cot.places, c_refs, pos, cbuf, sems, 0)
        first += tile_copies(w.places, w_refs, pos, wbuf, sems, len(first))
        later = wide_copies(x.places, x_refs, pos, xbuf, sems, len(first))
        n = len(first) + len(later)
        start(first)
        start(later)
        finish(first)

        def step(h, carry):
            lhs = far_blocks(cbuf, cols, down_order, h)
            rhs = jnp.concatenate([wbuf[down_order[h * K + k]] for k in range(K)], axis=1)
            pre[h] = (dot(lhs, rhs, (1, 1)) * slope[h]).astype(BF)
            return carry

        lax.fori_loop(0, H, step, 0, unroll=UNROLL)
        finish(later)

        def up_term(h, carry):
            lhs = far_blocks(xbuf, rows, up_order, h)
            out = dot(lhs, pre[h], (0, 0)).astype(BF)
            for k in range(K):
                at = grad_place(up_order[h * K + k], pos, False)
                up_terms[at] = out[k * B : (k + 1) * B]
            return carry

        lax.fori_loop(0, H, up_term, 0, unroll=UNROLL)
        up_copies = grad_copies(up_terms, ups, sems, n)
        start(up_copies)

        def down_term(h, carry):
            out = dot(hidden[h], far_blocks(cbuf, cols, down_order, h), (0, 0)).astype(BF)
            for k in range(K):
                at = grad_place(down_order[h * K + k], pos, True)
                down_terms[at] = out[:, k * B : (k + 1) * B]
            return carry

        lax.fori_loop(0, H, down_term, 0, unroll=UNROLL)
        down_copies = grad_copies(down_terms, downs, sems, n + 3)
        start(down_copies)
        finish(up_copies)
        finish(down_copies)

    n = len(cot.places) + len(w.places) + len(x.places) + 6
    out = call(
        kernel,
        [jax.ShapeDtypeStruct((H, B, B), BF)] + up_shapes + down_shapes,
        (down_order, cols, up_order, rows, pos),
        (*cot.arrays, *w.arrays, *x.arrays),
        (hidden, slope),
        [
            WIDE,
            TILES,
            WIDE,
            grad_scratch(False),
            grad_scratch(True),
            pltpu.SemaphoreType.DMA((n,)),
        ],
        out_specs=(VMEM_SPEC,) + (ANY_SPEC,) * 6,
        name="backward",
    )
    return out[0], out[1:4], out[4:]


RING = (0, 1, 2, 3, 6, 7)


def input_part(order, far, pos, act, w):
    def kernel(order, far, pos, *refs):
        nw = len(w.arrays)
        act, up, down, rest, wbuf, acc, sems = refs[nw:]
        copies = tile_copies(w.places, refs[:nw], pos, wbuf, sems, 0)
        start(copies)
        acc[...] = jnp.zeros_like(acc)
        finish(copies)

        def step(h, carry):
            js = [order[h * K + k] for k in range(K)]
            rhs = jnp.concatenate([wbuf[j] for j in js], axis=0)
            add_far(acc, far, js, dot(act[h], rhs, (1, 1)))
            return carry

        lax.fori_loop(0, H, step, 0, unroll=UNROLL)
        up[...] = acc[(pos[0] + 4) & 7].astype(BF)
        down[...] = acc[(pos[0] + 5) & 7].astype(BF)
        for n, r in enumerate(RING):
            rest[n] = acc[(pos[0] + r) & 7].astype(BF)

    one = jax.ShapeDtypeStruct((B, 8 * B), BF)
    return call(
        kernel,
        [one, one, jax.ShapeDtypeStruct((6, B, 8 * B), BF)],
        (order, far, pos),
        w.arrays,
        (act,),
        [TILES, WIDE_ACC, pltpu.SemaphoreType.DMA((len(w.places),))],
        name="input_part",
    )


def core_swap(a):
    return lax.ppermute(a, "fsdp", [(i, i ^ 1) for i in range(16)])


def y_swap(a):
    return lax.ppermute(a, "fsdp", [(i, i ^ 2) for i in range(16)])


def x_shift(a, d):
    return lax.ppermute(a, "fsdp", [(i, (i + 4 * d) % 16) for i in range(16)])


def dp_swap(a):
    return lax.ppermute(a, "dp", [(0, 1), (1, 0)])


def z_up(a):
    return lax.ppermute(a, "tensor", [(i, (i + 1) % 8) for i in range(8)])


def z_down(a):
    return lax.ppermute(a, "tensor", [(i, (i + 7) % 8) for i in range(8)])


def gather_up(tiles, *early):
    both = after(jnp.stack([tiles, y_swap(tiles)]), *early)
    mine = [both] + [x_shift(both, d) for d in (1, 3, 2)]
    arrays = mine + [core_swap(a) for a in mine]
    places = []
    for n in range(8):
        for dy in range(2):
            places.append((n, dy, ((0, 1, 3, 2)[n % 4], dy, n // 4)))
    return Wide(tuple(arrays), places)


def gather_down(tiles, early):
    x1, x3, x2 = (x_shift(tiles, d) for d in (1, 3, 2))
    mine = [jnp.stack([tiles, after(x1, early)]), jnp.stack([x3, after(x2, early)])]
    mine += [y_swap(a) for a in mine]
    arrays = mine + [core_swap(a) for a in mine]
    places = []
    for n in range(8):
        for i in range(2):
            places.append((n, i, ((0, 1, 3, 2)[n % 2 * 2 + i], n // 2 % 2, n // 4)))
    return Wide(tuple(arrays), places)


def add(a, b):
    return a.astype(F32) + b.astype(F32)


def scatter_features(partial):
    return lax.psum_scatter(partial, "tensor", scatter_dimension=0, tiled=True)[0]


def after(value, *others):
    return lax.optimization_barrier((value, *others))[0]


def body(activations, cotangent, up_tiles, down_tiles, up_rows, up_cols, down_rows, down_cols):
    f = lax.axis_index("fsdp")
    pos = jnp.stack([lax.axis_index("tensor"), f >> 2, (f >> 1) & 1, f & 1]).astype(jnp.int32)
    rows, cols = up_rows[:, 0], down_cols[:, 0]
    up_order, down_order = plan(up_cols[:, 0], down_rows[:, 0])
    pair = lax.all_gather(jnp.stack([activations, cotangent]), "tensor", axis=0, tiled=False)
    x = Wide((pair,), [(0, (z, 0), z, None) for z in range(8)])
    cot = Wide((pair,), [(0, (z, 1), z, None) for z in range(8)])
    up = gather_up(up_tiles, up_order, down_order, pos)
    down = gather_down(down_tiles, up.arrays[0])

    hidden, slope, partial_out = forward(up_order, rows, down_order, cols, pos, x, up, down)
    output = scatter_features(partial_out)
    pre_grad, (up0, up1, up_keep), (down12, down30, down_keep) = backward(
        down_order, cols, up_order, rows, pos, hidden, slope, cot, down, x
    )
    u1, u0 = core_swap(up1), core_swap(up0)
    near = add(up_keep[1], u1[0]).astype(BF)
    u_y = y_swap(near)
    d12, d30 = core_swap(down12), core_swap(down30)
    t1, t2 = add(down_keep[0], d12[0]).astype(BF), add(down_keep[1], d12[1]).astype(BF)
    d_x1 = x_shift(t1, 1)
    t3 = add(down_keep[2], d30[0]).astype(BF)
    d_x3 = x_shift(t3, 3)
    pre_grad_b = after(pre_grad, near, t1, t3)
    part4, part5, rest = input_part(up_order, rows, pos, pre_grad_b, up)

    part = {r: rest[n] for n, r in enumerate(RING)}
    part4, part5, _ = lax.optimization_barrier((part4, part5, (d_x1, d_x3)))
    z1, w1 = z_up(part4), z_down(part5)
    d_x2 = x_shift(after(t2, d_x1), 2)
    total = (add(up_keep[0], u0[0]) + u_y.astype(F32)).astype(BF)
    u_x1, u_x3 = x_shift(total[1], 1), x_shift(total[3], 3)
    z1, w1, _ = lax.optimization_barrier((z1, w1, total))
    z2, w2 = add(part[3], z1).astype(BF), add(part[6], w1).astype(BF)
    z2, w2, _ = lax.optimization_barrier((z2, w2, (output, d_x2)))
    z2, w2 = z_up(z2), z_down(w2)
    own = add(down_keep[3], d30[1]) + add(d_x1, d_x3) + d_x2.astype(F32)
    d_y = y_swap(own[1].astype(BF))
    u_x2 = x_shift(after(total[2], u_x1), 2)
    z3, w3 = add(part[2], z2).astype(BF), add(part[7], w2).astype(BF)
    z3, w3, _ = lax.optimization_barrier((z3, w3, (u_x1, u_x3)))
    z3, w3 = z_up(z3), z_down(w3)
    down_mine = (own[0] + d_y.astype(F32)).astype(BF)
    d_dp = dp_swap(down_mine)
    up_mine = (total[0].astype(F32) + add(u_x1, u_x3) + u_x2.astype(F32)).astype(BF)
    z4 = z_up(after(add(part[1], z3).astype(BF), w3, d_y, u_x2))
    u_dp = dp_swap(up_mine)
    input_grad = (part[0].astype(F32) + add(z4, w3)).astype(BF)
    return (output, input_grad, add(up_mine, u_dp), add(down_mine, d_dp))


def solution(mesh):
    in_specs = (
        P(("dp", "fsdp"), "tensor"),
        P(("dp", "fsdp"), "tensor"),
        P(("fsdp", "tensor"), None, None),
        P(("fsdp", "tensor"), None, None),
        P(None, "tensor"),
        P(None, "tensor"),
        P(None, "tensor"),
        P(None, "tensor"),
    )
    out_specs = (
        P(("dp", "fsdp"), "tensor"),
        P(("dp", "fsdp"), "tensor"),
        P(("fsdp", "tensor"), None, None),
        P(("fsdp", "tensor"), None, None),
    )
    return jax.shard_map(body, mesh=mesh, in_specs=in_specs, out_specs=out_specs, check_vma=False)
```

```python
import functools

import jax
import jax.numpy as jnp
from jax import lax
from jax.experimental import pallas as pl
from jax.experimental.pallas import tpu as pltpu
from jax.sharding import PartitionSpec as P

BF = jnp.bfloat16
F32 = jnp.float32
inv_root_two = 0.7071067811865476
inv_root_tau = 0.3989422804014327

B = 128
H = 16
K = 8
NT = 128
COST = 10_000_000
UNROLL = 2
VMEM_LIMIT = 56 * 1024 * 1024

SMEM_SPEC = pl.BlockSpec(memory_space=pltpu.SMEM)
VMEM_SPEC = pl.BlockSpec(memory_space=pltpu.VMEM)
ANY_SPEC = pl.BlockSpec(memory_space=pl.ANY)


def gelu_parts(values):
    normal_cdf = 0.5 * (1.0 + lax.erf(values * inv_root_two))
    density = inv_root_tau * jnp.exp(-0.5 * values * values)
    return (values * normal_cdf, normal_cdf + values * density)


def dot(a, b, dims):
    return lax.dot_general(a, b, ((dims[:1], dims[1:]), ((), ())), preferred_element_type=F32)


def plan_kernel(cols_ref, rows_ref, up_ref, down_ref, count):
    for near, order in ((cols_ref, up_ref), (rows_ref, down_ref)):
        for h in range(H):
            count[h] = 0

        def step(j, carry):
            h = near[j]
            c = count[h]
            order[h * K + c] = j
            count[h] = c + 1
            return carry

        lax.fori_loop(0, NT, step, 0)


def plan(cols, rows):
    shape = jax.ShapeDtypeStruct((NT,), jnp.int32)
    return pl.pallas_call(
        plan_kernel,
        out_shape=(shape, shape),
        in_specs=[SMEM_SPEC] * 2,
        out_specs=(SMEM_SPEC, SMEM_SPEC),
        scratch_shapes=[pltpu.SMEM((H,), jnp.int32)],
        name="plan",
    )(cols, rows)


def block(ref, f):
    return ref[f >> 3, :, pl.ds(pl.multiple_of((f & 7) * B, B), B)]


class Wide:
    def __init__(self, arrays, places):
        self.arrays, self.places = arrays, places


def wide_copies(places, refs, pos, buf, sems, first):
    copies = []
    for n, (which, index, shift, lines) in enumerate(places):
        slot = shift if isinstance(shift, int) else (pos[0] + shift[0]) & 7
        src = refs[which].at[index] if index is not None else refs[which]
        dst = buf.at[slot] if lines is None else buf.at[slot, pl.ds(*lines)]
        copies.append(pltpu.make_async_copy(src, dst, sems.at[first + n]))
    return copies


def tile_copies(places, refs, pos, buf, sems, first):
    copies = []
    for n, (which, index, (dx, dy, dc)) in enumerate(places):
        slot = ((pos[1] - dx) & 3) * 4 + (pos[2] ^ dy) * 2 + (pos[3] ^ dc)
        src = refs[which].at[index] if index is not None else refs[which]
        copies.append(
            pltpu.make_async_copy(src, buf.at[pl.ds(slot * 8, 8)], sems.at[first + n])
        )
    return copies


WIDE = pltpu.VMEM((8, B, 8 * B), BF)
TILES = pltpu.VMEM((NT, B, B), BF)
WIDE_ACC = pltpu.VMEM((8, B, 8 * B), F32)


def call(kernel, out_shape, smem, hbm, vmem, scratch, out_specs=None, name=None):
    n_out = len(out_shape)
    return pl.pallas_call(
        kernel,
        out_shape=tuple(out_shape),
        in_specs=[SMEM_SPEC] * len(smem) + [ANY_SPEC] * len(hbm) + [VMEM_SPEC] * len(vmem),
        out_specs=out_specs or (VMEM_SPEC,) * n_out,
        scratch_shapes=scratch,
        compiler_params=pltpu.CompilerParams(vmem_limit_bytes=VMEM_LIMIT),
        cost_estimate=pl.CostEstimate(flops=COST, bytes_accessed=COST // 100, transcendentals=0),
        name=name,
    )(*smem, *hbm, *vmem)


def start(copies):
    for c in copies:
        c.start()


def finish(copies):
    for c in copies:
        c.wait()


def far_blocks(buf, rows, order, h):
    return jnp.concatenate([block(buf, rows[order[h * K + k]]) for k in range(K)], axis=1)


def add_far(acc, far, js, term):
    for k, j in enumerate(js):
        f = far[j]
        at = (f >> 3, slice(None), pl.ds(pl.multiple_of((f & 7) * B, B), B))
        acc[at] += term[:, k * B : (k + 1) * B]


def add_far(acc, far, js, term):
    for k, j in enumerate(js):
        f = far[j]
        at = (f >> 3, slice(None), pl.ds(pl.multiple_of((f & 7) * B, B), B))
        acc[at] += term[:, k * B : (k + 1) * B]


def grad_shapes(x_first):
    n, m = (4, 2) if x_first else (2, 4)
    piece = jax.ShapeDtypeStruct((n // 2, m, 8, B, B), BF)
    return [piece] * 2 + [jax.ShapeDtypeStruct((n, m, 8, B, B), BF)]


def grad_scratch(x_first):
    n, m = (4, 2) if x_first else (2, 4)
    return pltpu.VMEM((2, n, m, 8, B, B), BF)


def grad_place(j, pos, x_first):
    dc, dx, dy = ((j >> 3) & 1) ^ pos[3], ((j >> 5) - pos[1]) & 3, ((j >> 4) & 1) ^ pos[2]
    return (dc, (dx + 3) & 3, dy, j & 7) if x_first else (dc, dy, dx, j & 7)


def grad_copies(grads, outs, sems, first):
    n = outs[0].shape[0]
    return [
        pltpu.make_async_copy(grads.at[1, pl.ds(0, n)], outs[0], sems.at[first]),
        pltpu.make_async_copy(grads.at[1, pl.ds(n, n)], outs[1], sems.at[first + 1]),
        pltpu.make_async_copy(grads.at[0], outs[2], sems.at[first + 2]),
    ]


RING = (0, 1, 2, 3, 6, 7)


def tile_pass(up_order, rows, down_order, cols, pos, x, cot, up, down):
    up_shapes, down_shapes = grad_shapes(False), grad_shapes(True)
    groups = (x.arrays, up.arrays, cot.arrays, down.arrays)
    counts = [len(g) for g in groups]

    def kernel(up_order, rows, down_order, cols, pos, *refs):
        ins, refs = refs[: sum(counts)], refs[sum(counts) :]
        x_refs, u_refs = ins[: counts[0]], ins[counts[0] : sum(counts[:2])]
        c_refs, d_refs = ins[sum(counts[:2]) : sum(counts[:3])], ins[sum(counts[:3]) :]
        ups, downs, (ring_up, ring_down, rest, out), scratch = refs[:3], refs[3:6], refs[6:10], refs[10:]
        xbuf, ubuf, cbuf, dbuf, hidden, slope, pre, up_terms, down_terms, acc, sems = scratch
        first = wide_copies(x.places, x_refs, pos, xbuf, sems, 0)
        first += tile_copies(up.places, u_refs, pos, ubuf, sems, len(first))
        later = wide_copies(cot.places, c_refs, pos, cbuf, sems, len(first))
        later += tile_copies(down.places, d_refs, pos, dbuf, sems, len(first) + len(later))
        n = len(first) + len(later)
        start(first)
        start(later)
        acc[...] = jnp.zeros_like(acc)
        finish(first)

        def forward(h, carry):
            lhs = far_blocks(xbuf, rows, up_order, h)
            rhs = jnp.concatenate([ubuf[up_order[h * K + k]] for k in range(K)], axis=0)
            act, der = gelu_parts(dot(lhs, rhs, (1, 0)))
            hidden[h] = act.astype(BF)
            slope[h] = der
            return carry

        lax.fori_loop(0, H, forward, 0, unroll=UNROLL)
        finish(later)

        def backward(h, carry):
            lhs = far_blocks(cbuf, cols, down_order, h)
            rhs = jnp.concatenate([dbuf[down_order[h * K + k]] for k in range(K)], axis=1)
            pre[h] = (dot(lhs, rhs, (1, 1)) * slope[h]).astype(BF)
            return carry

        lax.fori_loop(0, H, backward, 0, unroll=UNROLL)

        def up_term(h, carry):
            lhs = far_blocks(xbuf, rows, up_order, h)
            term = dot(lhs, pre[h], (0, 0)).astype(BF)
            for k in range(K):
                at = grad_place(up_order[h * K + k], pos, False)
                up_terms[at] = term[k * B : (k + 1) * B]
            return carry

        lax.fori_loop(0, H, up_term, 0, unroll=UNROLL)
        up_copies = grad_copies(up_terms, ups, sems, n)
        start(up_copies)

        def down_term(h, carry):
            term = dot(hidden[h], far_blocks(cbuf, cols, down_order, h), (0, 0)).astype(BF)
            for k in range(K):
                at = grad_place(down_order[h * K + k], pos, True)
                down_terms[at] = term[:, k * B : (k + 1) * B]
            return carry

        lax.fori_loop(0, H, down_term, 0, unroll=UNROLL)
        down_copies = grad_copies(down_terms, downs, sems, n + 3)
        start(down_copies)

        def input_part(h, carry):
            js = [up_order[h * K + k] for k in range(K)]
            rhs = jnp.concatenate([ubuf[j] for j in js], axis=0)
            add_far(acc, rows, js, dot(pre[h], rhs, (1, 1)))
            return carry

        lax.fori_loop(0, H, input_part, 0, unroll=UNROLL)
        ring_up[...] = acc[(pos[0] + 4) & 7].astype(BF)
        ring_down[...] = acc[(pos[0] + 5) & 7].astype(BF)
        for i, r in enumerate(RING):
            rest[i] = acc[(pos[0] + r) & 7].astype(BF)
        acc[...] = jnp.zeros_like(acc)

        def output_part(h, carry):
            js = [down_order[h * K + k] for k in range(K)]
            rhs = jnp.concatenate([dbuf[j] for j in js], axis=1)
            add_far(acc, cols, js, dot(hidden[h], rhs, (1, 0)))
            return carry

        lax.fori_loop(0, H, output_part, 0, unroll=UNROLL)
        out[...] = acc[...].astype(BF)
        finish(up_copies)
        finish(down_copies)

    n = len(x.places) + len(up.places) + len(cot.places) + len(down.places) + 6
    one = jax.ShapeDtypeStruct((B, 8 * B), BF)
    hiddens = (H, B, B)
    got = call(
        kernel,
        [
            *up_shapes,
            *down_shapes,
            one,
            one,
            jax.ShapeDtypeStruct((6, B, 8 * B), BF),
            jax.ShapeDtypeStruct((8, B, 8 * B), BF),
        ],
        (up_order, rows, down_order, cols, pos),
        sum(groups, ()),
        (),
        [
            WIDE,
            TILES,
            WIDE,
            TILES,
            pltpu.VMEM(hiddens, BF),
            pltpu.VMEM(hiddens, F32),
            pltpu.VMEM(hiddens, BF),
            grad_scratch(False),
            grad_scratch(True),
            WIDE_ACC,
            pltpu.SemaphoreType.DMA((n,)),
        ],
        out_specs=(ANY_SPEC,) * 6 + (VMEM_SPEC,) * 4,
        name="tile_pass",
    )
    return got[:3], got[3:6], got[6:9], got[9]


def core_swap(a):
    return lax.ppermute(a, "fsdp", [(i, i ^ 1) for i in range(16)])


def y_swap(a):
    return lax.ppermute(a, "fsdp", [(i, i ^ 2) for i in range(16)])


def x_shift(a, d):
    return lax.ppermute(a, "fsdp", [(i, (i + 4 * d) % 16) for i in range(16)])


def dp_swap(a):
    return lax.ppermute(a, "dp", [(0, 1), (1, 0)])


def z_up(a):
    return lax.ppermute(a, "tensor", [(i, (i + 1) % 8) for i in range(8)])


def z_down(a):
    return lax.ppermute(a, "tensor", [(i, (i + 7) % 8) for i in range(8)])


def gather_up(tiles, *early):
    both = after(jnp.stack([tiles, y_swap(tiles)]), *early)
    mine = [both] + [x_shift(both, d) for d in (1, 3, 2)]
    arrays = mine + [core_swap(a) for a in mine]
    places = []
    for n in range(8):
        for dy in range(2):
            places.append((n, dy, ((0, 1, 3, 2)[n % 4], dy, n // 4)))
    return Wide(tuple(arrays), places)


def gather_down(tiles, early):
    x1, x3, x2 = (x_shift(tiles, d) for d in (1, 3, 2))
    mine = [jnp.stack([tiles, after(x1, early)]), jnp.stack([x3, after(x2, early)])]
    mine += [y_swap(a) for a in mine]
    arrays = mine + [core_swap(a) for a in mine]
    places = []
    for n in range(8):
        for i in range(2):
            places.append((n, i, ((0, 1, 3, 2)[n % 2 * 2 + i], n // 2 % 2, n // 4)))
    return Wide(tuple(arrays), places)


def add(a, b):
    return a.astype(F32) + b.astype(F32)


def scatter_features(partial):
    return lax.psum_scatter(partial, "tensor", scatter_dimension=0, tiled=True)[0]


def after(value, *others):
    return lax.optimization_barrier((value, *others))[0]


def body(activations, cotangent, up_tiles, down_tiles, up_rows, up_cols, down_rows, down_cols):
    f = lax.axis_index("fsdp")
    pos = jnp.stack([lax.axis_index("tensor"), f >> 2, (f >> 1) & 1, f & 1]).astype(jnp.int32)
    rows, cols = up_rows[:, 0], down_cols[:, 0]
    up_order, down_order = plan(up_cols[:, 0], down_rows[:, 0])
    pair = lax.all_gather(jnp.stack([activations, cotangent]), "tensor", axis=0, tiled=False)
    x = Wide((pair,), [(0, (z, 0), z, None) for z in range(8)])
    cot = Wide((pair,), [(0, (z, 1), z, None) for z in range(8)])
    up = gather_up(up_tiles, up_order, down_order, pos)
    down = gather_down(down_tiles, up.arrays[0])

    (up0, up1, up_keep), (down12, down30, down_keep), ring_parts, partial_out = tile_pass(
        up_order, rows, down_order, cols, pos, x, cot, up, down
    )
    output = scatter_features(partial_out)
    u1 = core_swap(up1)
    near = add(up_keep[1], u1[0]).astype(BF)
    u_y = y_swap(near)
    d12, d30 = core_swap(down12), core_swap(down30)
    d12 = after(d12, near)
    t1, t2 = add(down_keep[0], d12[0]).astype(BF), add(down_keep[1], d12[1]).astype(BF)
    d_x1 = x_shift(t1, 1)
    t3 = add(down_keep[2], d30[0]).astype(BF)
    d_x3 = x_shift(t3, 3)
    u0 = core_swap(after(up0, d_x1))
    part4, part5, rest = ring_parts

    part = {r: rest[n] for n, r in enumerate(RING)}
    z1, w1 = z_up(part4), z_down(part5)
    d_x2 = x_shift(after(t2, d_x1), 2)
    total = (add(up_keep[0], u0[0]) + u_y.astype(F32)).astype(BF)
    u_x1, u_x3 = x_shift(total[1], 1), x_shift(total[3], 3)
    z1, w1, _ = lax.optimization_barrier((z1, w1, near))
    z2, w2 = add(part[3], z1).astype(BF), add(part[6], w1).astype(BF)
    z2, w2, _ = lax.optimization_barrier((z2, w2, (d_x2, total)))
    z2, w2 = z_up(z2), z_down(w2)
    own = add(down_keep[3], d30[1]) + add(d_x1, d_x3) + d_x2.astype(F32)
    d_y = y_swap(own[1].astype(BF))
    u_x2 = x_shift(total[2], 2)
    z3, w3 = add(part[2], z2).astype(BF), add(part[7], w2).astype(BF)
    z3, w3, _ = lax.optimization_barrier((z3, w3, (u_x1, u_x3)))
    z3, w3 = z_up(z3), z_down(w3)
    down_mine = (own[0] + d_y.astype(F32)).astype(BF)
    d_dp = dp_swap(down_mine)
    up_mine = (total[0].astype(F32) + add(u_x1, u_x3) + u_x2.astype(F32)).astype(BF)
    z4 = z_up(after(add(part[1], z3).astype(BF), w3, u_x2, output))
    u_dp = dp_swap(up_mine)
    input_grad = (part[0].astype(F32) + add(z4, w3)).astype(BF)
    return (output, input_grad, add(up_mine, u_dp), add(down_mine, d_dp))


def solution(mesh):
    in_specs = (
        P(("dp", "fsdp"), "tensor"),
        P(("dp", "fsdp"), "tensor"),
        P(("fsdp", "tensor"), None, None),
        P(("fsdp", "tensor"), None, None),
        P(None, "tensor"),
        P(None, "tensor"),
        P(None, "tensor"),
        P(None, "tensor"),
    )
    out_specs = (
        P(("dp", "fsdp"), "tensor"),
        P(("dp", "fsdp"), "tensor"),
        P(("fsdp", "tensor"), None, None),
        P(("fsdp", "tensor"), None, None),
    )
    return jax.shard_map(body, mesh=mesh, in_specs=in_specs, out_specs=out_specs, check_vma=False)
```

```python
import functools

import jax
import jax.numpy as jnp
from jax import lax
from jax.experimental import pallas as pl
from jax.experimental.pallas import tpu as pltpu
from jax.sharding import PartitionSpec as P

BF = jnp.bfloat16
F32 = jnp.float32
inv_root_two = 0.7071067811865476
inv_root_tau = 0.3989422804014327

B = 128
H = 16
K = 8
NT = 128
COST = 10_000_000
UNROLL = 4
VMEM_LIMIT = 56 * 1024 * 1024

SMEM_SPEC = pl.BlockSpec(memory_space=pltpu.SMEM)
VMEM_SPEC = pl.BlockSpec(memory_space=pltpu.VMEM)
ANY_SPEC = pl.BlockSpec(memory_space=pl.ANY)


def gelu_parts(values):
    normal_cdf = 0.5 * (1.0 + lax.erf(values * inv_root_two))
    density = inv_root_tau * jnp.exp(-0.5 * values * values)
    return (values * normal_cdf, normal_cdf + values * density)


def dot(a, b, dims):
    return lax.dot_general(a, b, ((dims[:1], dims[1:]), ((), ())), preferred_element_type=F32)


def plan_kernel(cols_ref, rows_ref, up_ref, down_ref, count):
    for near, order in ((cols_ref, up_ref), (rows_ref, down_ref)):
        for h in range(H):
            count[h] = 0

        def step(j, carry):
            h = near[j]
            c = count[h]
            order[h * K + c] = j
            count[h] = c + 1
            return carry

        lax.fori_loop(0, NT, step, 0)


def plan(cols, rows):
    shape = jax.ShapeDtypeStruct((NT,), jnp.int32)
    return pl.pallas_call(
        plan_kernel,
        out_shape=(shape, shape),
        in_specs=[SMEM_SPEC] * 2,
        out_specs=(SMEM_SPEC, SMEM_SPEC),
        scratch_shapes=[pltpu.SMEM((H,), jnp.int32)],
        name="plan",
    )(cols, rows)


def block(ref, f):
    return ref[f >> 3, :, pl.ds(pl.multiple_of((f & 7) * B, B), B)]


class Wide:
    def __init__(self, arrays, places):
        self.arrays, self.places = arrays, places


def wide_copies(places, refs, pos, buf, sems, first):
    copies = []
    for n, (which, index, shift, lines) in enumerate(places):
        slot = shift if isinstance(shift, int) else (pos[0] + shift[0]) & 7
        src = refs[which].at[index] if index is not None else refs[which]
        dst = buf.at[slot] if lines is None else buf.at[slot, pl.ds(*lines)]
        copies.append(pltpu.make_async_copy(src, dst, sems.at[first + n]))
    return copies


def tile_copies(places, refs, pos, buf, sems, first):
    copies = []
    for n, (which, index, (dx, dy, dc)) in enumerate(places):
        slot = ((pos[1] - dx) & 3) * 4 + (pos[2] ^ dy) * 2 + (pos[3] ^ dc)
        src = refs[which].at[index] if index is not None else refs[which]
        copies.append(
            pltpu.make_async_copy(src, buf.at[pl.ds(slot * 8, 8)], sems.at[first + n])
        )
    return copies


WIDE = pltpu.VMEM((8, B, 8 * B), BF)
TILES = pltpu.VMEM((NT, B, B), BF)
WIDE_ACC = pltpu.VMEM((8, B, 8 * B), F32)


def call(kernel, out_shape, smem, hbm, vmem, scratch, out_specs=None, name=None):
    n_out = len(out_shape)
    return pl.pallas_call(
        kernel,
        out_shape=tuple(out_shape),
        in_specs=[SMEM_SPEC] * len(smem) + [ANY_SPEC] * len(hbm) + [VMEM_SPEC] * len(vmem),
        out_specs=out_specs or (VMEM_SPEC,) * n_out,
        scratch_shapes=scratch,
        compiler_params=pltpu.CompilerParams(vmem_limit_bytes=VMEM_LIMIT),
        cost_estimate=pl.CostEstimate(flops=COST, bytes_accessed=COST // 100, transcendentals=0),
        name=name,
    )(*smem, *hbm, *vmem)


def start(copies):
    for c in copies:
        c.start()


def finish(copies):
    for c in copies:
        c.wait()


def far_blocks(buf, rows, order, h):
    return jnp.concatenate([block(buf, rows[order[h * K + k]]) for k in range(K)], axis=1)


def add_far(acc, far, js, term):
    for k, j in enumerate(js):
        f = far[j]
        at = (f >> 3, slice(None), pl.ds(pl.multiple_of((f & 7) * B, B), B))
        acc[at] += term[:, k * B : (k + 1) * B]


def add_far(acc, far, js, term):
    for k, j in enumerate(js):
        f = far[j]
        at = (f >> 3, slice(None), pl.ds(pl.multiple_of((f & 7) * B, B), B))
        acc[at] += term[:, k * B : (k + 1) * B]


def grad_shapes(x_first):
    n, m = (4, 2) if x_first else (2, 4)
    piece = jax.ShapeDtypeStruct((n // 2, m, 8, B, B), BF)
    return [piece] * 2 + [jax.ShapeDtypeStruct((n, m, 8, B, B), BF)]


def grad_scratch(x_first):
    n, m = (4, 2) if x_first else (2, 4)
    return pltpu.VMEM((2, n, m, 8, B, B), BF)


def grad_place(j, pos, x_first):
    dc, dx, dy = ((j >> 3) & 1) ^ pos[3], ((j >> 5) - pos[1]) & 3, ((j >> 4) & 1) ^ pos[2]
    return (dc, (dx + 3) & 3, dy, j & 7) if x_first else (dc, dy, dx, j & 7)


def grad_copies(grads, outs, sems, first):
    n = outs[0].shape[0]
    return [
        pltpu.make_async_copy(grads.at[1, pl.ds(0, n)], outs[0], sems.at[first]),
        pltpu.make_async_copy(grads.at[1, pl.ds(n, n)], outs[1], sems.at[first + 1]),
        pltpu.make_async_copy(grads.at[0], outs[2], sems.at[first + 2]),
    ]


def tile_pass(up_order, rows, down_order, cols, pos, x, cot, up, down):
    up_shapes, down_shapes = grad_shapes(False), grad_shapes(True)
    groups = (x.arrays, up.arrays, cot.arrays, down.arrays)
    counts = [len(g) for g in groups]

    def kernel(up_order, rows, down_order, cols, pos, *refs):
        ins, refs = refs[: sum(counts)], refs[sum(counts) :]
        x_refs, u_refs = ins[: counts[0]], ins[counts[0] : sum(counts[:2])]
        c_refs, d_refs = ins[sum(counts[:2]) : sum(counts[:3])], ins[sum(counts[:3]) :]
        ups, downs, parts, scratch = refs[:3], refs[3:6], refs[6], refs[7:]
        xbuf, ubuf, cbuf, dbuf, hidden, slope, pre, up_terms, down_terms, acc, sems = scratch
        first = wide_copies(x.places, x_refs, pos, xbuf, sems, 0)
        first += tile_copies(up.places, u_refs, pos, ubuf, sems, len(first))
        later = wide_copies(cot.places, c_refs, pos, cbuf, sems, len(first))
        later += tile_copies(down.places, d_refs, pos, dbuf, sems, len(first) + len(later))
        n = len(first) + len(later)
        start(first)
        start(later)
        acc[...] = jnp.zeros_like(acc)
        finish(first)

        def forward(h, carry):
            lhs = far_blocks(xbuf, rows, up_order, h)
            rhs = jnp.concatenate([ubuf[up_order[h * K + k]] for k in range(K)], axis=0)
            act, der = gelu_parts(dot(lhs, rhs, (1, 0)))
            hidden[h] = act.astype(BF)
            slope[h] = der
            return carry

        lax.fori_loop(0, H, forward, 0, unroll=UNROLL)
        finish(later)

        def backward(h, carry):
            lhs = far_blocks(cbuf, cols, down_order, h)
            rhs = jnp.concatenate([dbuf[down_order[h * K + k]] for k in range(K)], axis=1)
            pre[h] = (dot(lhs, rhs, (1, 1)) * slope[h]).astype(BF)
            return carry

        lax.fori_loop(0, H, backward, 0, unroll=UNROLL)

        def up_term(h, carry):
            lhs = far_blocks(xbuf, rows, up_order, h)
            term = dot(lhs, pre[h], (0, 0)).astype(BF)
            for k in range(K):
                at = grad_place(up_order[h * K + k], pos, False)
                up_terms[at] = term[k * B : (k + 1) * B]
            return carry

        lax.fori_loop(0, H, up_term, 0, unroll=UNROLL)
        up_copies = grad_copies(up_terms, ups, sems, n)
        start(up_copies)

        def down_term(h, carry):
            term = dot(hidden[h], far_blocks(cbuf, cols, down_order, h), (0, 0)).astype(BF)
            for k in range(K):
                at = grad_place(down_order[h * K + k], pos, True)
                down_terms[at] = term[:, k * B : (k + 1) * B]
            return carry

        lax.fori_loop(0, H, down_term, 0, unroll=UNROLL)
        down_copies = grad_copies(down_terms, downs, sems, n + 3)
        start(down_copies)

        def input_part(h, carry):
            js = [up_order[h * K + k] for k in range(K)]
            rhs = jnp.concatenate([ubuf[j] for j in js], axis=0)
            add_far(acc, rows, js, dot(pre[h], rhs, (1, 1)))
            return carry

        lax.fori_loop(0, H, input_part, 0, unroll=UNROLL)
        parts[:, 1] = acc[...].astype(BF)
        acc[...] = jnp.zeros_like(acc)

        def output_part(h, carry):
            js = [down_order[h * K + k] for k in range(K)]
            rhs = jnp.concatenate([dbuf[j] for j in js], axis=1)
            add_far(acc, cols, js, dot(hidden[h], rhs, (1, 0)))
            return carry

        lax.fori_loop(0, H, output_part, 0, unroll=UNROLL)
        parts[:, 0] = acc[...].astype(BF)
        finish(up_copies)
        finish(down_copies)

    n = len(x.places) + len(up.places) + len(cot.places) + len(down.places) + 6
    hiddens = (H, B, B)
    got = call(
        kernel,
        [
            *up_shapes,
            *down_shapes,
            jax.ShapeDtypeStruct((8, 2, B, 8 * B), BF),
        ],
        (up_order, rows, down_order, cols, pos),
        sum(groups, ()),
        (),
        [
            WIDE,
            TILES,
            WIDE,
            TILES,
            pltpu.VMEM(hiddens, BF),
            pltpu.VMEM(hiddens, F32),
            pltpu.VMEM(hiddens, BF),
            grad_scratch(False),
            grad_scratch(True),
            WIDE_ACC,
            pltpu.SemaphoreType.DMA((n,)),
        ],
        out_specs=(ANY_SPEC,) * 6 + (VMEM_SPEC,),
        name="tile_pass",
    )
    return got[:3], got[3:6], got[6]


def core_swap(a):
    return lax.ppermute(a, "fsdp", [(i, i ^ 1) for i in range(16)])


def y_swap(a):
    return lax.ppermute(a, "fsdp", [(i, i ^ 2) for i in range(16)])


def x_shift(a, d):
    return lax.ppermute(a, "fsdp", [(i, (i + 4 * d) % 16) for i in range(16)])


def dp_swap(a):
    return lax.ppermute(a, "dp", [(0, 1), (1, 0)])


def gather_up(tiles, *early):
    both = after(jnp.stack([tiles, y_swap(tiles)]), *early)
    mine = [both] + [x_shift(both, d) for d in (1, 3, 2)]
    arrays = mine + [core_swap(a) for a in mine]
    places = []
    for n in range(8):
        for dy in range(2):
            places.append((n, dy, ((0, 1, 3, 2)[n % 4], dy, n // 4)))
    return Wide(tuple(arrays), places)


def gather_down(tiles, early):
    x1, x3, x2 = (x_shift(tiles, d) for d in (1, 3, 2))
    mine = [jnp.stack([tiles, after(x1, early)]), jnp.stack([x3, after(x2, early)])]
    mine += [y_swap(a) for a in mine]
    arrays = mine + [core_swap(a) for a in mine]
    places = []
    for n in range(8):
        for i in range(2):
            places.append((n, i, ((0, 1, 3, 2)[n % 2 * 2 + i], n // 2 % 2, n // 4)))
    return Wide(tuple(arrays), places)


def add(a, b):
    return a.astype(F32) + b.astype(F32)


def scatter_features(partial):
    return lax.psum_scatter(partial, "tensor", scatter_dimension=0, tiled=True)[0]


def after(value, *others):
    return lax.optimization_barrier((value, *others))[0]


def body(activations, cotangent, up_tiles, down_tiles, up_rows, up_cols, down_rows, down_cols):
    f = lax.axis_index("fsdp")
    pos = jnp.stack([lax.axis_index("tensor"), f >> 2, (f >> 1) & 1, f & 1]).astype(jnp.int32)
    rows, cols = up_rows[:, 0], down_cols[:, 0]
    up_order, down_order = plan(up_cols[:, 0], down_rows[:, 0])
    pair = lax.all_gather(jnp.stack([activations, cotangent]), "tensor", axis=0, tiled=False)
    x = Wide((pair,), [(0, (z, 0), z, None) for z in range(8)])
    cot = Wide((pair,), [(0, (z, 1), z, None) for z in range(8)])
    up = gather_up(up_tiles, up_order, down_order, pos)
    down = gather_down(down_tiles, up.arrays[0])

    (up0, up1, up_keep), (down12, down30, down_keep), parts = tile_pass(
        up_order, rows, down_order, cols, pos, x, cot, up, down
    )
    output, input_grad = scatter_features(parts)
    u1, d12, d30 = core_swap(up1), core_swap(down12), core_swap(down30)
    near = add(up_keep[1], u1[0]).astype(BF)
    u_y = y_swap(near)
    d12 = after(d12, near)
    t1, t2 = add(down_keep[0], d12[0]).astype(BF), add(down_keep[1], d12[1]).astype(BF)
    t3 = add(down_keep[2], d30[0]).astype(BF)
    d_x1, d_x3, d_x2 = x_shift(t1, 1), x_shift(t3, 3), x_shift(t2, 2)
    u0 = core_swap(after(up0, d_x1))
    total = (add(up_keep[0], u0[0]) + u_y.astype(F32)).astype(BF)
    u_x1, u_x3, u_x2 = x_shift(total[1], 1), x_shift(total[3], 3), x_shift(total[2], 2)
    own = add(down_keep[3], d30[1]) + add(d_x1, d_x3) + d_x2.astype(F32)
    d_y = y_swap(own[1].astype(BF))
    down_mine = (own[0] + d_y.astype(F32)).astype(BF)
    d_dp = dp_swap(down_mine)
    up_mine = (total[0].astype(F32) + add(u_x1, u_x3) + u_x2.astype(F32)).astype(BF)
    u_dp = dp_swap(up_mine)
    return (output, input_grad, add(up_mine, u_dp), add(down_mine, d_dp))


def solution(mesh):
    in_specs = (
        P(("dp", "fsdp"), "tensor"),
        P(("dp", "fsdp"), "tensor"),
        P(("fsdp", "tensor"), None, None),
        P(("fsdp", "tensor"), None, None),
        P(None, "tensor"),
        P(None, "tensor"),
        P(None, "tensor"),
        P(None, "tensor"),
    )
    out_specs = (
        P(("dp", "fsdp"), "tensor"),
        P(("dp", "fsdp"), "tensor"),
        P(("fsdp", "tensor"), None, None),
        P(("fsdp", "tensor"), None, None),
    )
    return jax.shard_map(body, mesh=mesh, in_specs=in_specs, out_specs=out_specs, check_vma=False)
```

```python
import functools

import jax
import jax.numpy as jnp
from jax import lax
from jax.experimental import pallas as pl
from jax.experimental.pallas import tpu as pltpu
from jax.sharding import PartitionSpec as P

BF = jnp.bfloat16
F32 = jnp.float32
inv_root_two = 0.7071067811865476
inv_root_tau = 0.3989422804014327

B = 128
H = 16
K = 8
NT = 128
COST = 10_000_000
UNROLL = 4
VMEM_LIMIT = 56 * 1024 * 1024

SMEM_SPEC = pl.BlockSpec(memory_space=pltpu.SMEM)
VMEM_SPEC = pl.BlockSpec(memory_space=pltpu.VMEM)
ANY_SPEC = pl.BlockSpec(memory_space=pl.ANY)


def gelu_parts(values):
    normal_cdf = 0.5 * (1.0 + lax.erf(values * inv_root_two))
    density = inv_root_tau * jnp.exp(-0.5 * values * values)
    return (values * normal_cdf, normal_cdf + values * density)


def dot(a, b, dims):
    return lax.dot_general(a, b, ((dims[:1], dims[1:]), ((), ())), preferred_element_type=F32)


def plan_kernel(cols_ref, rows_ref, up_ref, down_ref, count):
    for near, order in ((cols_ref, up_ref), (rows_ref, down_ref)):
        for h in range(H):
            count[h] = 0

        def step(j, carry):
            h = near[j]
            c = count[h]
            order[h * K + c] = j
            count[h] = c + 1
            return carry

        lax.fori_loop(0, NT, step, 0)


def plan(cols, rows):
    shape = jax.ShapeDtypeStruct((NT,), jnp.int32)
    return pl.pallas_call(
        plan_kernel,
        out_shape=(shape, shape),
        in_specs=[SMEM_SPEC] * 2,
        out_specs=(SMEM_SPEC, SMEM_SPEC),
        scratch_shapes=[pltpu.SMEM((H,), jnp.int32)],
        name="plan",
    )(cols, rows)


def block(ref, f):
    return ref[f >> 3, :, pl.ds(pl.multiple_of((f & 7) * B, B), B)]


class Wide:
    def __init__(self, arrays, places):
        self.arrays, self.places = arrays, places


def wide_copies(places, refs, pos, buf, sems, first):
    copies = []
    for n, (which, index, shift, lines) in enumerate(places):
        slot = shift if isinstance(shift, int) else (pos[0] + shift[0]) & 7
        src = refs[which].at[index] if index is not None else refs[which]
        dst = buf.at[slot] if lines is None else buf.at[slot, pl.ds(*lines)]
        copies.append(pltpu.make_async_copy(src, dst, sems.at[first + n]))
    return copies


def tile_copies(places, refs, pos, buf, sems, first):
    copies = []
    for n, (which, index, (dx, dy, dc)) in enumerate(places):
        slot = ((pos[1] - dx) & 3) * 4 + (pos[2] ^ dy) * 2 + (pos[3] ^ dc)
        src = refs[which].at[index] if index is not None else refs[which]
        copies.append(
            pltpu.make_async_copy(src, buf.at[pl.ds(slot * 8, 8)], sems.at[first + n])
        )
    return copies


WIDE = pltpu.VMEM((8, B, 8 * B), BF)
TILES = pltpu.VMEM((NT, B, B), BF)
WIDE_ACC = pltpu.VMEM((8, B, 8 * B), F32)


def call(kernel, out_shape, smem, hbm, vmem, scratch, out_specs=None, name=None):
    n_out = len(out_shape)
    return pl.pallas_call(
        kernel,
        out_shape=tuple(out_shape),
        in_specs=[SMEM_SPEC] * len(smem) + [ANY_SPEC] * len(hbm) + [VMEM_SPEC] * len(vmem),
        out_specs=out_specs or (VMEM_SPEC,) * n_out,
        scratch_shapes=scratch,
        compiler_params=pltpu.CompilerParams(vmem_limit_bytes=VMEM_LIMIT),
        cost_estimate=pl.CostEstimate(flops=COST, bytes_accessed=COST // 100, transcendentals=0),
        name=name,
    )(*smem, *hbm, *vmem)


def start(copies):
    for c in copies:
        c.start()


def finish(copies):
    for c in copies:
        c.wait()


def far_blocks(buf, rows, order, h):
    return jnp.concatenate([block(buf, rows[order[h * K + k]]) for k in range(K)], axis=1)


def add_far(acc, far, js, term):
    for k, j in enumerate(js):
        f = far[j]
        at = (f >> 3, slice(None), pl.ds(pl.multiple_of((f & 7) * B, B), B))
        acc[at] += term[:, k * B : (k + 1) * B]


def add_far(acc, far, js, term):
    for k, j in enumerate(js):
        f = far[j]
        at = (f >> 3, slice(None), pl.ds(pl.multiple_of((f & 7) * B, B), B))
        acc[at] += term[:, k * B : (k + 1) * B]


def grad_shapes(x_first):
    n, m = (4, 2) if x_first else (2, 4)
    piece = jax.ShapeDtypeStruct((n // 2, m, 8, B, B), BF)
    return [piece] * 2 + [jax.ShapeDtypeStruct((n, m, 8, B, B), BF)]


def grad_scratch(x_first):
    n, m = (4, 2) if x_first else (2, 4)
    return pltpu.VMEM((2, n, m, 8, B, B), BF)


def grad_place(j, pos, x_first):
    dc, dx, dy = ((j >> 3) & 1) ^ pos[3], ((j >> 5) - pos[1]) & 3, ((j >> 4) & 1) ^ pos[2]
    return (dc, (dx + 3) & 3, dy, j & 7) if x_first else (dc, dy, dx, j & 7)


def grad_copies(grads, outs, sems, first):
    n = outs[0].shape[0]
    return [
        pltpu.make_async_copy(grads.at[1, pl.ds(0, n)], outs[0], sems.at[first]),
        pltpu.make_async_copy(grads.at[1, pl.ds(n, n)], outs[1], sems.at[first + 1]),
        pltpu.make_async_copy(grads.at[0], outs[2], sems.at[first + 2]),
    ]


def tile_pass(up_order, rows, down_order, cols, pos, x, cot, up, down):
    up_shapes, down_shapes = grad_shapes(False), grad_shapes(True)
    groups = (x.arrays, up.arrays, cot.arrays, down.arrays)
    counts = [len(g) for g in groups]

    def kernel(up_order, rows, down_order, cols, pos, *refs):
        ins, refs = refs[: sum(counts)], refs[sum(counts) :]
        x_refs, u_refs = ins[: counts[0]], ins[counts[0] : sum(counts[:2])]
        c_refs, d_refs = ins[sum(counts[:2]) : sum(counts[:3])], ins[sum(counts[:3]) :]
        ups, downs, parts, scratch = refs[:3], refs[3:6], refs[6], refs[7:]
        xbuf, ubuf, cbuf, dbuf, hidden, slope, pre, up_terms, down_terms, acc, sems = scratch
        first = wide_copies(x.places, x_refs, pos, xbuf, sems, 0)
        first += tile_copies(up.places, u_refs, pos, ubuf, sems, len(first))
        later = wide_copies(cot.places, c_refs, pos, cbuf, sems, len(first))
        later += tile_copies(down.places, d_refs, pos, dbuf, sems, len(first) + len(later))
        n = len(first) + len(later)
        start(first)
        start(later)
        acc[...] = jnp.zeros_like(acc)
        finish(first)

        def forward(h, carry):
            lhs = far_blocks(xbuf, rows, up_order, h)
            rhs = jnp.concatenate([ubuf[up_order[h * K + k]] for k in range(K)], axis=0)
            act, der = gelu_parts(dot(lhs, rhs, (1, 0)))
            hidden[h] = act.astype(BF)
            slope[h] = der
            return carry

        lax.fori_loop(0, H, forward, 0, unroll=UNROLL)
        finish(later)

        def backward(h, carry):
            lhs = far_blocks(cbuf, cols, down_order, h)
            rhs = jnp.concatenate([dbuf[down_order[h * K + k]] for k in range(K)], axis=1)
            pre[h] = (dot(lhs, rhs, (1, 1)) * slope[h]).astype(BF)
            return carry

        lax.fori_loop(0, H, backward, 0, unroll=UNROLL)

        def up_term(h, carry):
            lhs = far_blocks(xbuf, rows, up_order, h)
            term = dot(lhs, pre[h], (0, 0)).astype(BF)
            for k in range(K):
                at = grad_place(up_order[h * K + k], pos, False)
                up_terms[at] = term[k * B : (k + 1) * B]
            return carry

        lax.fori_loop(0, H, up_term, 0, unroll=UNROLL)
        up_copies = grad_copies(up_terms, ups, sems, n)
        start(up_copies)

        def down_term(h, carry):
            term = dot(hidden[h], far_blocks(cbuf, cols, down_order, h), (0, 0)).astype(BF)
            for k in range(K):
                at = grad_place(down_order[h * K + k], pos, True)
                down_terms[at] = term[:, k * B : (k + 1) * B]
            return carry

        lax.fori_loop(0, H, down_term, 0, unroll=UNROLL)
        down_copies = grad_copies(down_terms, downs, sems, n + 3)
        start(down_copies)

        def input_part(h, carry):
            js = [up_order[h * K + k] for k in range(K)]
            rhs = jnp.concatenate([ubuf[j] for j in js], axis=0)
            add_far(acc, rows, js, dot(pre[h], rhs, (1, 1)))
            return carry

        lax.fori_loop(0, H, input_part, 0, unroll=UNROLL)
        parts[:, 1] = acc[...].astype(BF)
        acc[...] = jnp.zeros_like(acc)

        def output_part(h, carry):
            js = [down_order[h * K + k] for k in range(K)]
            rhs = jnp.concatenate([dbuf[j] for j in js], axis=1)
            add_far(acc, cols, js, dot(hidden[h], rhs, (1, 0)))
            return carry

        lax.fori_loop(0, H, output_part, 0, unroll=UNROLL)
        parts[:, 0] = acc[...].astype(BF)
        finish(up_copies)
        finish(down_copies)

    n = len(x.places) + len(up.places) + len(cot.places) + len(down.places) + 6
    hiddens = (H, B, B)
    got = call(
        kernel,
        [
            *up_shapes,
            *down_shapes,
            jax.ShapeDtypeStruct((8, 2, B, 8 * B), BF),
        ],
        (up_order, rows, down_order, cols, pos),
        sum(groups, ()),
        (),
        [
            WIDE,
            TILES,
            WIDE,
            TILES,
            pltpu.VMEM(hiddens, BF),
            pltpu.VMEM(hiddens, F32),
            pltpu.VMEM(hiddens, BF),
            grad_scratch(False),
            grad_scratch(True),
            WIDE_ACC,
            pltpu.SemaphoreType.DMA((n,)),
        ],
        out_specs=(ANY_SPEC,) * 6 + (VMEM_SPEC,),
        name="tile_pass",
    )
    return got[:3], got[3:6], got[6]


def core_swap(a):
    return lax.ppermute(a, "fsdp", [(i, i ^ 1) for i in range(16)])


def y_swap(a):
    return lax.ppermute(a, "fsdp", [(i, i ^ 2) for i in range(16)])


def x_shift(a, d):
    return lax.ppermute(a, "fsdp", [(i, (i + 4 * d) % 16) for i in range(16)])


def dp_swap(a):
    return lax.ppermute(a, "dp", [(0, 1), (1, 0)])


def gather_up(tiles, *early):
    both = after(jnp.stack([tiles, y_swap(tiles)]), *early)
    mine = [both] + [x_shift(both, d) for d in (1, 3, 2)]
    arrays = mine + [core_swap(a) for a in mine]
    places = []
    for n in range(8):
        for dy in range(2):
            places.append((n, dy, ((0, 1, 3, 2)[n % 4], dy, n // 4)))
    return Wide(tuple(arrays), places)


def gather_down(tiles, early):
    x1, x3, x2 = (x_shift(tiles, d) for d in (1, 3, 2))
    mine = [jnp.stack([tiles, after(x1, early)]), jnp.stack([x3, after(x2, early)])]
    mine += [y_swap(a) for a in mine]
    arrays = mine + [core_swap(a) for a in mine]
    places = []
    for n in range(8):
        for i in range(2):
            places.append((n, i, ((0, 1, 3, 2)[n % 2 * 2 + i], n // 2 % 2, n // 4)))
    return Wide(tuple(arrays), places)


def add(a, b):
    return a.astype(F32) + b.astype(F32)


def scatter_features(partial):
    return lax.psum_scatter(partial, "tensor", scatter_dimension=0, tiled=True)[0]


def after(value, *others):
    return lax.optimization_barrier((value, *others))[0]


def body(activations, cotangent, up_tiles, down_tiles, up_rows, up_cols, down_rows, down_cols):
    f = lax.axis_index("fsdp")
    pos = jnp.stack([lax.axis_index("tensor"), f >> 2, (f >> 1) & 1, f & 1]).astype(jnp.int32)
    rows, cols = up_rows[:, 0], down_cols[:, 0]
    up_order, down_order = plan(up_cols[:, 0], down_rows[:, 0])
    pair = lax.all_gather(jnp.stack([activations, cotangent]), "tensor", axis=0, tiled=False)
    x = Wide((pair,), [(0, (z, 0), z, None) for z in range(8)])
    cot = Wide((pair,), [(0, (z, 1), z, None) for z in range(8)])
    up = gather_up(up_tiles, up_order, down_order, pos)
    down = gather_down(down_tiles, up.arrays[0])

    (up0, up1, up_keep), (down12, down30, down_keep), parts = tile_pass(
        up_order, rows, down_order, cols, pos, x, cot, up, down
    )
    output, input_grad = scatter_features(parts)
    u1, d12, d30 = core_swap(up1), core_swap(down12), core_swap(down30)
    near = add(up_keep[1], u1[0]).astype(BF)
    u_y = y_swap(near)
    u0 = core_swap(after(up0, near))
    d12, d30, _ = lax.optimization_barrier((d12, d30, u0))
    t1, t2 = add(down_keep[0], d12[0]).astype(BF), add(down_keep[1], d12[1]).astype(BF)
    t3 = add(down_keep[2], d30[0]).astype(BF)
    d_x1, d_x3, d_x2 = x_shift(t1, 1), x_shift(t3, 3), x_shift(t2, 2)
    total = (add(up_keep[0], u0[0]) + u_y.astype(F32)).astype(BF)
    u_x1, u_x3, u_x2 = x_shift(total[1], 1), x_shift(total[3], 3), x_shift(total[2], 2)
    own = add(down_keep[3], d30[1]) + add(d_x1, d_x3) + d_x2.astype(F32)
    d_y = y_swap(after(own[1].astype(BF), total))
    down_mine = (own[0] + d_y.astype(F32)).astype(BF)
    d_dp = dp_swap(down_mine)
    up_mine = (total[0].astype(F32) + add(u_x1, u_x3) + u_x2.astype(F32)).astype(BF)
    u_dp = after(dp_swap(up_mine), output, input_grad)
    return (output, input_grad, add(up_mine, u_dp), add(down_mine, d_dp))


def solution(mesh):
    in_specs = (
        P(("dp", "fsdp"), "tensor"),
        P(("dp", "fsdp"), "tensor"),
        P(("fsdp", "tensor"), None, None),
        P(("fsdp", "tensor"), None, None),
        P(None, "tensor"),
        P(None, "tensor"),
        P(None, "tensor"),
        P(None, "tensor"),
    )
    out_specs = (
        P(("dp", "fsdp"), "tensor"),
        P(("dp", "fsdp"), "tensor"),
        P(("fsdp", "tensor"), None, None),
        P(("fsdp", "tensor"), None, None),
    )
    return jax.shard_map(body, mesh=mesh, in_specs=in_specs, out_specs=out_specs, check_vma=False)
```

```python
import functools

import jax
import jax.numpy as jnp
from jax import lax
from jax.experimental import pallas as pl
from jax.experimental.pallas import tpu as pltpu
from jax.sharding import PartitionSpec as P

BF = jnp.bfloat16
F32 = jnp.float32
inv_root_two = 0.7071067811865476
inv_root_tau = 0.3989422804014327

B = 128
H = 16
K = 8
NT = 128
COST = 10_000_000
UNROLL = 4
VMEM_LIMIT = 56 * 1024 * 1024

SMEM_SPEC = pl.BlockSpec(memory_space=pltpu.SMEM)
VMEM_SPEC = pl.BlockSpec(memory_space=pltpu.VMEM)
ANY_SPEC = pl.BlockSpec(memory_space=pl.ANY)


def gelu_parts(values):
    normal_cdf = 0.5 * (1.0 + lax.erf(values * inv_root_two))
    density = inv_root_tau * jnp.exp(-0.5 * values * values)
    return (values * normal_cdf, normal_cdf + values * density)


def dot(a, b, dims):
    return lax.dot_general(a, b, ((dims[:1], dims[1:]), ((), ())), preferred_element_type=F32)


def plan_kernel(cols_ref, rows_ref, up_ref, down_ref, count):
    for near, order in ((cols_ref, up_ref), (rows_ref, down_ref)):
        for h in range(H):
            count[h] = 0

        def step(j, carry):
            h = near[j]
            c = count[h]
            order[h * K + c] = j
            count[h] = c + 1
            return carry

        lax.fori_loop(0, NT, step, 0)


def plan(cols, rows):
    shape = jax.ShapeDtypeStruct((NT,), jnp.int32)
    return pl.pallas_call(
        plan_kernel,
        out_shape=(shape, shape),
        in_specs=[SMEM_SPEC] * 2,
        out_specs=(SMEM_SPEC, SMEM_SPEC),
        scratch_shapes=[pltpu.SMEM((H,), jnp.int32)],
        name="plan",
    )(cols, rows)


def block(ref, f):
    return ref[f >> 3, :, pl.ds(pl.multiple_of((f & 7) * B, B), B)]


class Wide:
    def __init__(self, arrays, places):
        self.arrays, self.places = arrays, places


def wide_copies(places, refs, pos, buf, sems, first):
    copies = []
    for n, (which, index, shift, lines) in enumerate(places):
        slot = shift if isinstance(shift, int) else (pos[0] + shift[0]) & 7
        src = refs[which].at[index] if index is not None else refs[which]
        dst = buf.at[slot] if lines is None else buf.at[slot, pl.ds(*lines)]
        copies.append(pltpu.make_async_copy(src, dst, sems.at[first + n]))
    return copies


def tile_copies(places, refs, pos, buf, sems, first):
    copies = []
    for n, (which, index, (dx, dy, dc)) in enumerate(places):
        slot = ((pos[1] - dx) & 3) * 4 + (pos[2] ^ dy) * 2 + (pos[3] ^ dc)
        src = refs[which].at[index] if index is not None else refs[which]
        copies.append(
            pltpu.make_async_copy(src, buf.at[pl.ds(slot * 8, 8)], sems.at[first + n])
        )
    return copies


WIDE = pltpu.VMEM((8, B, 8 * B), BF)
TILES = pltpu.VMEM((NT, B, B), BF)
WIDE_ACC = pltpu.VMEM((8, B, 8 * B), F32)


def call(kernel, out_shape, smem, hbm, vmem, scratch, out_specs=None, name=None):
    n_out = len(out_shape)
    return pl.pallas_call(
        kernel,
        out_shape=tuple(out_shape),
        in_specs=[SMEM_SPEC] * len(smem) + [ANY_SPEC] * len(hbm) + [VMEM_SPEC] * len(vmem),
        out_specs=out_specs or (VMEM_SPEC,) * n_out,
        scratch_shapes=scratch,
        compiler_params=pltpu.CompilerParams(vmem_limit_bytes=VMEM_LIMIT),
        cost_estimate=pl.CostEstimate(flops=COST, bytes_accessed=COST // 100, transcendentals=0),
        name=name,
    )(*smem, *hbm, *vmem)


def start(copies):
    for c in copies:
        c.start()


def finish(copies):
    for c in copies:
        c.wait()


def far_blocks(buf, rows, order, h):
    return jnp.concatenate([block(buf, rows[order[h * K + k]]) for k in range(K)], axis=1)


def add_far(acc, far, js, term):
    for k, j in enumerate(js):
        f = far[j]
        at = (f >> 3, slice(None), pl.ds(pl.multiple_of((f & 7) * B, B), B))
        acc[at] += term[:, k * B : (k + 1) * B]


def add_far(acc, far, js, term):
    for k, j in enumerate(js):
        f = far[j]
        at = (f >> 3, slice(None), pl.ds(pl.multiple_of((f & 7) * B, B), B))
        acc[at] += term[:, k * B : (k + 1) * B]


def grad_shapes(x_first):
    n, m = (4, 2) if x_first else (2, 4)
    piece = jax.ShapeDtypeStruct((n // 2, m, 8, B, B), BF)
    return [piece] * 2 + [jax.ShapeDtypeStruct((n, m, 8, B, B), BF)]


def grad_scratch(x_first):
    n, m = (4, 2) if x_first else (2, 4)
    return pltpu.VMEM((2, n, m, 8, B, B), BF)


def grad_place(j, pos, x_first):
    dc, dx, dy = ((j >> 3) & 1) ^ pos[3], ((j >> 5) - pos[1]) & 3, ((j >> 4) & 1) ^ pos[2]
    return (dc, (dx + 3) & 3, dy, j & 7) if x_first else (dc, dy, dx, j & 7)


def grad_copies(grads, outs, sems, first):
    n = outs[0].shape[0]
    return [
        pltpu.make_async_copy(grads.at[1, pl.ds(0, n)], outs[0], sems.at[first]),
        pltpu.make_async_copy(grads.at[1, pl.ds(n, n)], outs[1], sems.at[first + 1]),
        pltpu.make_async_copy(grads.at[0], outs[2], sems.at[first + 2]),
    ]


def tile_pass(up_order, rows, down_order, cols, pos, x, cot, up, down):
    up_shapes, down_shapes = grad_shapes(False), grad_shapes(True)
    groups = (x.arrays, up.arrays, cot.arrays, down.arrays)
    counts = [len(g) for g in groups]

    def kernel(up_order, rows, down_order, cols, pos, *refs):
        ins, refs = refs[: sum(counts)], refs[sum(counts) :]
        x_refs, u_refs = ins[: counts[0]], ins[counts[0] : sum(counts[:2])]
        c_refs, d_refs = ins[sum(counts[:2]) : sum(counts[:3])], ins[sum(counts[:3]) :]
        ups, downs, parts, scratch = refs[:3], refs[3:6], refs[6], refs[7:]
        xbuf, ubuf, cbuf, dbuf, hidden, slope, pre, up_terms, down_terms, acc, sems = scratch
        first = wide_copies(x.places, x_refs, pos, xbuf, sems, 0)
        first += tile_copies(up.places, u_refs, pos, ubuf, sems, len(first))
        later = wide_copies(cot.places, c_refs, pos, cbuf, sems, len(first))
        later += tile_copies(down.places, d_refs, pos, dbuf, sems, len(first) + len(later))
        n = len(first) + len(later)
        start(first)
        start(later)
        acc[...] = jnp.zeros_like(acc)
        finish(first)

        def forward(h, carry):
            lhs = far_blocks(xbuf, rows, up_order, h)
            rhs = jnp.concatenate([ubuf[up_order[h * K + k]] for k in range(K)], axis=0)
            act, der = gelu_parts(dot(lhs, rhs, (1, 0)))
            hidden[h] = act.astype(BF)
            slope[h] = der
            return carry

        lax.fori_loop(0, H, forward, 0, unroll=UNROLL)
        finish(later)

        def backward(h, carry):
            lhs = far_blocks(cbuf, cols, down_order, h)
            rhs = jnp.concatenate([dbuf[down_order[h * K + k]] for k in range(K)], axis=1)
            pre[h] = (dot(lhs, rhs, (1, 1)) * slope[h]).astype(BF)
            return carry

        lax.fori_loop(0, H, backward, 0, unroll=UNROLL)

        def up_term(h, carry):
            lhs = far_blocks(xbuf, rows, up_order, h)
            term = dot(lhs, pre[h], (0, 0)).astype(BF)
            for k in range(K):
                at = grad_place(up_order[h * K + k], pos, False)
                up_terms[at] = term[k * B : (k + 1) * B]
            return carry

        lax.fori_loop(0, H, up_term, 0, unroll=UNROLL)
        up_copies = grad_copies(up_terms, ups, sems, n)
        start(up_copies)

        def down_term(h, carry):
            term = dot(hidden[h], far_blocks(cbuf, cols, down_order, h), (0, 0)).astype(BF)
            for k in range(K):
                at = grad_place(down_order[h * K + k], pos, True)
                down_terms[at] = term[:, k * B : (k + 1) * B]
            return carry

        lax.fori_loop(0, H, down_term, 0, unroll=UNROLL)
        down_copies = grad_copies(down_terms, downs, sems, n + 3)
        start(down_copies)

        def input_part(h, carry):
            js = [up_order[h * K + k] for k in range(K)]
            rhs = jnp.concatenate([ubuf[j] for j in js], axis=0)
            add_far(acc, rows, js, dot(pre[h], rhs, (1, 1)))
            return carry

        lax.fori_loop(0, H, input_part, 0, unroll=UNROLL)
        parts[:, 1] = acc[...].astype(BF)
        acc[...] = jnp.zeros_like(acc)

        def output_part(h, carry):
            js = [down_order[h * K + k] for k in range(K)]
            rhs = jnp.concatenate([dbuf[j] for j in js], axis=1)
            add_far(acc, cols, js, dot(hidden[h], rhs, (1, 0)))
            return carry

        lax.fori_loop(0, H, output_part, 0, unroll=UNROLL)
        parts[:, 0] = acc[...].astype(BF)
        finish(up_copies)
        finish(down_copies)

    n = len(x.places) + len(up.places) + len(cot.places) + len(down.places) + 6
    hiddens = (H, B, B)
    got = call(
        kernel,
        [
            *up_shapes,
            *down_shapes,
            jax.ShapeDtypeStruct((8, 2, B, 8 * B), BF),
        ],
        (up_order, rows, down_order, cols, pos),
        sum(groups, ()),
        (),
        [
            WIDE,
            TILES,
            WIDE,
            TILES,
            pltpu.VMEM(hiddens, BF),
            pltpu.VMEM(hiddens, F32),
            pltpu.VMEM(hiddens, BF),
            grad_scratch(False),
            grad_scratch(True),
            WIDE_ACC,
            pltpu.SemaphoreType.DMA((n,)),
        ],
        out_specs=(ANY_SPEC,) * 6 + (VMEM_SPEC,),
        name="tile_pass",
    )
    return got[:3], got[3:6], got[6]


def core_swap(a):
    return lax.ppermute(a, "fsdp", [(i, i ^ 1) for i in range(16)])


def y_swap(a):
    return lax.ppermute(a, "fsdp", [(i, i ^ 2) for i in range(16)])


def x_shift(a, d):
    return lax.ppermute(a, "fsdp", [(i, (i + 4 * d) % 16) for i in range(16)])


def dp_swap(a):
    return lax.ppermute(a, "dp", [(0, 1), (1, 0)])


def z_up(a):
    return lax.ppermute(a, "tensor", [(i, (i + 1) % 8) for i in range(8)])


def z_down(a):
    return lax.ppermute(a, "tensor", [(i, (i + 7) % 8) for i in range(8)])


def ring_gather(a, *before_last):
    arrays, places = [a], [(0, None, (0,), None)]
    up = down = a
    for k in (1, 2, 3, 4):
        up = z_up(up if k < 4 else after(up, *before_last))
        down = z_down(down) if k < 4 else None
        for part, shift in ((up, -k), (down, k)):
            if part is not None:
                places.append((len(arrays), None, (shift,), None))
                arrays.append(part)
    return Wide(tuple(arrays), places)


def gather_up(tiles, *early):
    both = after(jnp.stack([tiles, y_swap(tiles)]), *early)
    mine = [both] + [x_shift(both, d) for d in (1, 3, 2)]
    arrays = mine + [core_swap(a) for a in mine]
    places = []
    for n in range(8):
        for dy in range(2):
            places.append((n, dy, ((0, 1, 3, 2)[n % 4], dy, n // 4)))
    return Wide(tuple(arrays), places)


def gather_down(tiles, early):
    x1, x3, x2 = (x_shift(tiles, d) for d in (1, 3, 2))
    mine = [jnp.stack([tiles, after(x1, early)]), jnp.stack([x3, after(x2, early)])]
    mine += [y_swap(a) for a in mine]
    arrays = mine + [core_swap(a) for a in mine]
    places = []
    for n in range(8):
        for i in range(2):
            places.append((n, i, ((0, 1, 3, 2)[n % 2 * 2 + i], n // 2 % 2, n // 4)))
    return Wide(tuple(arrays), places)


def add(a, b):
    return a.astype(F32) + b.astype(F32)


def scatter_features(partial):
    return lax.psum_scatter(partial, "tensor", scatter_dimension=0, tiled=True)[0]


def after(value, *others):
    return lax.optimization_barrier((value, *others))[0]


def body(activations, cotangent, up_tiles, down_tiles, up_rows, up_cols, down_rows, down_cols):
    f = lax.axis_index("fsdp")
    pos = jnp.stack([lax.axis_index("tensor"), f >> 2, (f >> 1) & 1, f & 1]).astype(jnp.int32)
    rows, cols = up_rows[:, 0], down_cols[:, 0]
    up_order, down_order = plan(up_cols[:, 0], down_rows[:, 0])
    wide = lax.all_gather(cotangent, "tensor", axis=0, tiled=False)
    cot = Wide((wide,), [(0, z, z, None) for z in range(8)])
    up = gather_up(up_tiles, up_order, down_order, pos)
    down = gather_down(down_tiles, up.arrays[0])
    x = ring_gather(activations, *up.arrays[1:3], *down.arrays[2:4])

    (up0, up1, up_keep), (down12, down30, down_keep), parts = tile_pass(
        up_order, rows, down_order, cols, pos, x, cot, up, down
    )
    output, input_grad = scatter_features(parts)
    u1, d12, d30 = core_swap(up1), core_swap(down12), core_swap(down30)
    near = add(up_keep[1], u1[0]).astype(BF)
    u_y = y_swap(near)
    u0 = core_swap(after(up0, near))
    d12, d30, _ = lax.optimization_barrier((d12, d30, u0))
    t1, t2 = add(down_keep[0], d12[0]).astype(BF), add(down_keep[1], d12[1]).astype(BF)
    t3 = add(down_keep[2], d30[0]).astype(BF)
    d_x1, d_x3, d_x2 = x_shift(t1, 1), x_shift(t3, 3), x_shift(t2, 2)
    total = (add(up_keep[0], u0[0]) + u_y.astype(F32)).astype(BF)
    u_x1, u_x3, u_x2 = x_shift(total[1], 1), x_shift(total[3], 3), x_shift(total[2], 2)
    own = add(down_keep[3], d30[1]) + add(d_x1, d_x3) + d_x2.astype(F32)
    d_y = y_swap(after(own[1].astype(BF), total))
    down_mine = (own[0] + d_y.astype(F32)).astype(BF)
    d_dp = dp_swap(down_mine)
    up_mine = (total[0].astype(F32) + add(u_x1, u_x3) + u_x2.astype(F32)).astype(BF)
    u_dp = after(dp_swap(up_mine), output, input_grad)
    return (output, input_grad, add(up_mine, u_dp), add(down_mine, d_dp))


def solution(mesh):
    in_specs = (
        P(("dp", "fsdp"), "tensor"),
        P(("dp", "fsdp"), "tensor"),
        P(("fsdp", "tensor"), None, None),
        P(("fsdp", "tensor"), None, None),
        P(None, "tensor"),
        P(None, "tensor"),
        P(None, "tensor"),
        P(None, "tensor"),
    )
    out_specs = (
        P(("dp", "fsdp"), "tensor"),
        P(("dp", "fsdp"), "tensor"),
        P(("fsdp", "tensor"), None, None),
        P(("fsdp", "tensor"), None, None),
    )
    return jax.shard_map(body, mesh=mesh, in_specs=in_specs, out_specs=out_specs, check_vma=False)
```

```python
import functools

import jax
import jax.numpy as jnp
from jax import lax
from jax.experimental import pallas as pl
from jax.experimental.pallas import tpu as pltpu
from jax.sharding import PartitionSpec as P

BF = jnp.bfloat16
F32 = jnp.float32
inv_root_two = 0.7071067811865476
inv_root_tau = 0.3989422804014327

B = 128
H = 16
K = 8
NT = 128
COST = 10_000_000
UNROLL = 4
VMEM_LIMIT = 56 * 1024 * 1024

SMEM_SPEC = pl.BlockSpec(memory_space=pltpu.SMEM)
VMEM_SPEC = pl.BlockSpec(memory_space=pltpu.VMEM)
ANY_SPEC = pl.BlockSpec(memory_space=pl.ANY)


def gelu_parts(values):
    normal_cdf = 0.5 * (1.0 + lax.erf(values * inv_root_two))
    density = inv_root_tau * jnp.exp(-0.5 * values * values)
    return (values * normal_cdf, normal_cdf + values * density)


def dot(a, b, dims):
    return lax.dot_general(a, b, ((dims[:1], dims[1:]), ((), ())), preferred_element_type=F32)


def plan_kernel(cols_ref, rows_ref, up_ref, down_ref, count):
    for near, order in ((cols_ref, up_ref), (rows_ref, down_ref)):
        for h in range(H):
            count[h] = 0

        def step(j, carry):
            h = near[j]
            c = count[h]
            order[h * K + c] = j
            count[h] = c + 1
            return carry

        lax.fori_loop(0, NT, step, 0)


def plan(cols, rows):
    shape = jax.ShapeDtypeStruct((NT,), jnp.int32)
    return pl.pallas_call(
        plan_kernel,
        out_shape=(shape, shape),
        in_specs=[SMEM_SPEC] * 2,
        out_specs=(SMEM_SPEC, SMEM_SPEC),
        scratch_shapes=[pltpu.SMEM((H,), jnp.int32)],
        name="plan",
    )(cols, rows)


def block(ref, f):
    return ref[f >> 3, :, pl.ds(pl.multiple_of((f & 7) * B, B), B)]


class Wide:
    def __init__(self, arrays, places):
        self.arrays, self.places = arrays, places


def wide_copies(places, refs, pos, buf, sems, first):
    copies = []
    for n, (which, index, shift, lines) in enumerate(places):
        slot = shift if isinstance(shift, int) else (pos[0] + shift[0]) & 7
        src = refs[which].at[index] if index is not None else refs[which]
        dst = buf.at[slot] if lines is None else buf.at[slot, pl.ds(*lines)]
        copies.append(pltpu.make_async_copy(src, dst, sems.at[first + n]))
    return copies


def tile_copies(places, refs, pos, buf, sems, first):
    copies = []
    for n, (which, index, (dx, dy, dc)) in enumerate(places):
        slot = ((pos[1] - dx) & 3) * 4 + (pos[2] ^ dy) * 2 + (pos[3] ^ dc)
        src = refs[which].at[index] if index is not None else refs[which]
        copies.append(
            pltpu.make_async_copy(src, buf.at[pl.ds(slot * 8, 8)], sems.at[first + n])
        )
    return copies


WIDE = pltpu.VMEM((8, B, 8 * B), BF)
TILES = pltpu.VMEM((NT, B, B), BF)
WIDE_ACC = pltpu.VMEM((8, B, 8 * B), F32)


def call(kernel, out_shape, smem, hbm, vmem, scratch, out_specs=None, name=None):
    n_out = len(out_shape)
    return pl.pallas_call(
        kernel,
        out_shape=tuple(out_shape),
        in_specs=[SMEM_SPEC] * len(smem) + [ANY_SPEC] * len(hbm) + [VMEM_SPEC] * len(vmem),
        out_specs=out_specs or (VMEM_SPEC,) * n_out,
        scratch_shapes=scratch,
        compiler_params=pltpu.CompilerParams(vmem_limit_bytes=VMEM_LIMIT),
        cost_estimate=pl.CostEstimate(flops=COST, bytes_accessed=COST // 100, transcendentals=0),
        name=name,
    )(*smem, *hbm, *vmem)


def start(copies):
    for c in copies:
        c.start()


def finish(copies):
    for c in copies:
        c.wait()


def far_blocks(buf, rows, order, h):
    return jnp.concatenate([block(buf, rows[order[h * K + k]]) for k in range(K)], axis=1)


def add_far(acc, far, js, term):
    for k, j in enumerate(js):
        f = far[j]
        at = (f >> 3, slice(None), pl.ds(pl.multiple_of((f & 7) * B, B), B))
        acc[at] += term[:, k * B : (k + 1) * B]


def add_far(acc, far, js, term):
    for k, j in enumerate(js):
        f = far[j]
        at = (f >> 3, slice(None), pl.ds(pl.multiple_of((f & 7) * B, B), B))
        acc[at] += term[:, k * B : (k + 1) * B]


def grad_shapes(x_first):
    n, m = (4, 2) if x_first else (2, 4)
    piece = jax.ShapeDtypeStruct((n // 2, m, 8, B, B), BF)
    return [piece] * 2 + [jax.ShapeDtypeStruct((n, m, 8, B, B), BF)]


def grad_scratch(x_first):
    n, m = (4, 2) if x_first else (2, 4)
    return pltpu.VMEM((2, n, m, 8, B, B), BF)


def grad_place(j, pos, x_first):
    dc, dx, dy = ((j >> 3) & 1) ^ pos[3], ((j >> 5) - pos[1]) & 3, ((j >> 4) & 1) ^ pos[2]
    return (dc, (dx + 3) & 3, dy, j & 7) if x_first else (dc, dy, dx, j & 7)


def grad_copies(grads, outs, sems, first):
    n = outs[0].shape[0]
    return [
        pltpu.make_async_copy(grads.at[1, pl.ds(0, n)], outs[0], sems.at[first]),
        pltpu.make_async_copy(grads.at[1, pl.ds(n, n)], outs[1], sems.at[first + 1]),
        pltpu.make_async_copy(grads.at[0], outs[2], sems.at[first + 2]),
    ]


def tile_pass(up_order, rows, down_order, cols, pos, x, cot, up, down):
    up_shapes, down_shapes = grad_shapes(False), grad_shapes(True)
    groups = (x.arrays, up.arrays, cot.arrays, down.arrays)
    counts = [len(g) for g in groups]

    def kernel(up_order, rows, down_order, cols, pos, *refs):
        ins, refs = refs[: sum(counts)], refs[sum(counts) :]
        x_refs, u_refs = ins[: counts[0]], ins[counts[0] : sum(counts[:2])]
        c_refs, d_refs = ins[sum(counts[:2]) : sum(counts[:3])], ins[sum(counts[:3]) :]
        ups, downs, parts, scratch = refs[:3], refs[3:6], refs[6], refs[7:]
        xbuf, ubuf, cbuf, dbuf, hidden, slope, pre, up_terms, down_terms, acc, sems = scratch
        first = wide_copies(x.places, x_refs, pos, xbuf, sems, 0)
        first += tile_copies(up.places, u_refs, pos, ubuf, sems, len(first))
        later = wide_copies(cot.places, c_refs, pos, cbuf, sems, len(first))
        later += tile_copies(down.places, d_refs, pos, dbuf, sems, len(first) + len(later))
        n = len(first) + len(later)
        start(first)
        start(later)
        acc[...] = jnp.zeros_like(acc)
        finish(first)

        def forward(h, carry):
            lhs = far_blocks(xbuf, rows, up_order, h)
            rhs = jnp.concatenate([ubuf[up_order[h * K + k]] for k in range(K)], axis=0)
            act, der = gelu_parts(dot(lhs, rhs, (1, 0)))
            hidden[h] = act.astype(BF)
            slope[h] = der
            return carry

        lax.fori_loop(0, H, forward, 0, unroll=UNROLL)
        finish(later)

        def backward(h, carry):
            lhs = far_blocks(cbuf, cols, down_order, h)
            rhs = jnp.concatenate([dbuf[down_order[h * K + k]] for k in range(K)], axis=1)
            pre[h] = (dot(lhs, rhs, (1, 1)) * slope[h]).astype(BF)
            return carry

        lax.fori_loop(0, H, backward, 0, unroll=UNROLL)

        def up_term(h, carry):
            lhs = far_blocks(xbuf, rows, up_order, h)
            term = dot(lhs, pre[h], (0, 0)).astype(BF)
            for k in range(K):
                at = grad_place(up_order[h * K + k], pos, False)
                up_terms[at] = term[k * B : (k + 1) * B]
            return carry

        lax.fori_loop(0, H, up_term, 0, unroll=UNROLL)
        up_copies = grad_copies(up_terms, ups, sems, n)
        start(up_copies)

        def down_term(h, carry):
            term = dot(hidden[h], far_blocks(cbuf, cols, down_order, h), (0, 0)).astype(BF)
            for k in range(K):
                at = grad_place(down_order[h * K + k], pos, True)
                down_terms[at] = term[:, k * B : (k + 1) * B]
            return carry

        lax.fori_loop(0, H, down_term, 0, unroll=UNROLL)
        down_copies = grad_copies(down_terms, downs, sems, n + 3)
        start(down_copies)

        def input_part(h, carry):
            js = [up_order[h * K + k] for k in range(K)]
            rhs = jnp.concatenate([ubuf[j] for j in js], axis=0)
            add_far(acc, rows, js, dot(pre[h], rhs, (1, 1)))
            return carry

        lax.fori_loop(0, H, input_part, 0, unroll=UNROLL)
        parts[:, 1] = acc[...].astype(BF)
        acc[...] = jnp.zeros_like(acc)

        def output_part(h, carry):
            js = [down_order[h * K + k] for k in range(K)]
            rhs = jnp.concatenate([dbuf[j] for j in js], axis=1)
            add_far(acc, cols, js, dot(hidden[h], rhs, (1, 0)))
            return carry

        lax.fori_loop(0, H, output_part, 0, unroll=UNROLL)
        parts[:, 0] = acc[...].astype(BF)
        finish(up_copies)
        finish(down_copies)

    n = len(x.places) + len(up.places) + len(cot.places) + len(down.places) + 6
    hiddens = (H, B, B)
    got = call(
        kernel,
        [
            *up_shapes,
            *down_shapes,
            jax.ShapeDtypeStruct((8, 2, B, 8 * B), BF),
        ],
        (up_order, rows, down_order, cols, pos),
        sum(groups, ()),
        (),
        [
            WIDE,
            TILES,
            WIDE,
            TILES,
            pltpu.VMEM(hiddens, BF),
            pltpu.VMEM(hiddens, F32),
            pltpu.VMEM(hiddens, BF),
            grad_scratch(False),
            grad_scratch(True),
            WIDE_ACC,
            pltpu.SemaphoreType.DMA((n,)),
        ],
        out_specs=(ANY_SPEC,) * 6 + (VMEM_SPEC,),
        name="tile_pass",
    )
    return got[:3], got[3:6], got[6]


def core_swap(a):
    return lax.ppermute(a, "fsdp", [(i, i ^ 1) for i in range(16)])


def y_swap(a):
    return lax.ppermute(a, "fsdp", [(i, i ^ 2) for i in range(16)])


def x_shift(a, d):
    return lax.ppermute(a, "fsdp", [(i, (i + 4 * d) % 16) for i in range(16)])


def dp_swap(a):
    return lax.ppermute(a, "dp", [(0, 1), (1, 0)])


def gather_up(tiles, *early):
    both = after(jnp.stack([tiles, y_swap(tiles)]), *early)
    mine = [both] + [x_shift(both, d) for d in (1, 3, 2)]
    arrays = mine + [core_swap(a) for a in mine]
    places = []
    for n in range(8):
        for dy in range(2):
            places.append((n, dy, ((0, 1, 3, 2)[n % 4], dy, n // 4)))
    return Wide(tuple(arrays), places)


def gather_down(tiles, early):
    x1, x3, x2 = (x_shift(tiles, d) for d in (1, 3, 2))
    mine = [jnp.stack([tiles, after(x1, early)]), jnp.stack([x3, after(x2, early)])]
    mine += [y_swap(a) for a in mine]
    arrays = mine + [core_swap(a) for a in mine]
    places = []
    for n in range(8):
        for i in range(2):
            places.append((n, i, ((0, 1, 3, 2)[n % 2 * 2 + i], n // 2 % 2, n // 4)))
    return Wide(tuple(arrays), places)


def add(a, b):
    return a.astype(F32) + b.astype(F32)


def scatter_features(partial):
    return lax.psum_scatter(partial, "tensor", scatter_dimension=0, tiled=True)[0]


def after(value, *others):
    return lax.optimization_barrier((value, *others))[0]


def body(activations, cotangent, up_tiles, down_tiles, up_rows, up_cols, down_rows, down_cols):
    f = lax.axis_index("fsdp")
    pos = jnp.stack([lax.axis_index("tensor"), f >> 2, (f >> 1) & 1, f & 1]).astype(jnp.int32)
    rows, cols = up_rows[:, 0], down_cols[:, 0]
    up_order, down_order = plan(up_cols[:, 0], down_rows[:, 0])
    pair = lax.all_gather(jnp.stack([activations, cotangent]), "tensor", axis=0, tiled=False)
    x = Wide((pair,), [(0, (z, 0), z, None) for z in range(8)])
    cot = Wide((pair,), [(0, (z, 1), z, None) for z in range(8)])
    up = gather_up(up_tiles, up_order, down_order, pos)
    down = gather_down(down_tiles, up.arrays[0])

    (up0, up1, up_keep), (down12, down30, down_keep), parts = tile_pass(
        up_order, rows, down_order, cols, pos, x, cot, up, down
    )
    output, input_grad = scatter_features(parts)
    u1, d12, d30 = core_swap(up1), core_swap(down12), core_swap(down30)
    near = add(up_keep[1], u1[0]).astype(BF)
    u_y = y_swap(near)
    u0 = core_swap(after(up0, near))
    d12, d30, _ = lax.optimization_barrier((d12, d30, u0))
    t1, t2 = add(down_keep[0], d12[0]).astype(BF), add(down_keep[1], d12[1]).astype(BF)
    t3 = add(down_keep[2], d30[0]).astype(BF)
    d_x1, d_x3, d_x2 = x_shift(t1, 1), x_shift(t3, 3), x_shift(t2, 2)
    total = (add(up_keep[0], u0[0]) + u_y.astype(F32)).astype(BF)
    u_x1, u_x3, u_x2 = x_shift(total[1], 1), x_shift(total[3], 3), x_shift(total[2], 2)
    own = add(down_keep[3], d30[1]) + add(d_x1, d_x3) + d_x2.astype(F32)
    d_y = y_swap(after(own[1].astype(BF), total, u_x1, u_x3))
    down_mine = (own[0] + d_y.astype(F32)).astype(BF)
    d_dp = dp_swap(down_mine)
    up_mine = (total[0].astype(F32) + add(u_x1, u_x3) + u_x2.astype(F32)).astype(BF)
    u_dp = after(dp_swap(up_mine), output, input_grad)
    return (output, input_grad, add(up_mine, u_dp), add(down_mine, d_dp))


def solution(mesh):
    in_specs = (
        P(("dp", "fsdp"), "tensor"),
        P(("dp", "fsdp"), "tensor"),
        P(("fsdp", "tensor"), None, None),
        P(("fsdp", "tensor"), None, None),
        P(None, "tensor"),
        P(None, "tensor"),
        P(None, "tensor"),
        P(None, "tensor"),
    )
    out_specs = (
        P(("dp", "fsdp"), "tensor"),
        P(("dp", "fsdp"), "tensor"),
        P(("fsdp", "tensor"), None, None),
        P(("fsdp", "tensor"), None, None),
    )
    return jax.shard_map(body, mesh=mesh, in_specs=in_specs, out_specs=out_specs, check_vma=False)
```
